512 devices in a mesh: rad: 32 (over z, core), ord: 16 (over y, x).
Axes of the slice: x: 4, y: 4, z: 16, core: 2. Of those that a mesh axis runs over, the one named last changes fastest.
Arguments:
- coefficients: bfloat16 [4, 256, 256, 2, 256], P(None, 'rad', 'ord'), may hold values from -0.05859375 to 0.05859375
- order_of_slot: int32 [256], replicated, may hold values from 0 to 255, as said below
Outputs:
- grid: bfloat16 [4, 2, 256, 384, 768], P(None, None, 'rad', 'ord')
The draws below stay inside these ranges and needn't reach their ends.
Inputs may be any that keep to these rules, and one draw needn't show every extreme that they name: `order_of_slot`: each order 0 to 255 stands in exactly one slot; slots 2i and 2i+1 hold two orders that sum to 255.
All inputs are finite; a program needn't handle non-finite values.
Results may differ from the reference program's by a relative error of at most 0.0016.
Values may be sent and summed in bfloat16 or wider, within the bound.
A program may use at most 128 MiB of HBM per device.

```python
import math
import jax
import jax.numpy as jnp
from jax import lax

LDEG = 256
NLAT = 384
NLON = 768
POT = 4
R_DEV = 8
NR = 256
N_RAD = 32


def draw_order_of_slot(key, part):
    first_key, second_key = jax.random.split(jax.random.fold_in(key, 7))
    pair_heads = jax.random.permutation(first_key, LDEG // 2).astype(jnp.int32)
    flipped = jax.random.randint(second_key, (LDEG // 2,), 0, 2, dtype=jnp.int32)
    leading = jnp.where(flipped == 1, LDEG - 1 - pair_heads, pair_heads)
    return jnp.stack([leading, LDEG - 1 - leading], axis=1).reshape(LDEG)


def levels(key, extent, shards, low, high):
    def one(position, parts):
        draws = jax.random.uniform(jax.random.fold_in(jax.random.fold_in(key, 6), position), (parts,), jnp.float32, low / len(shards), high / len(shards))
        return jnp.repeat(jnp.exp(draws), extent[position] // parts).reshape((-1,) + (1,) * (len(extent) - position - 1))

    gain = one(*shards[0])
    for cut in shards[1:]:
        gain = gain * one(*cut)
    return gain


def bell_draw(key, extent, spread, reach, pieces=(), kind=jnp.bfloat16):
    drawn = spread * jax.random.normal(key, extent, jnp.float32)
    if pieces:
        drawn = drawn * levels(key, extent, pieces, -0.22, 0.18)
    return jnp.clip(drawn, -reach, reach).astype(kind)


def setup_inputs(seed: int = 0) -> dict:
    key_list = jax.random.split(jax.random.key(seed), 3)
    return {
        "coefficients": bell_draw(key_list[0], (POT, NR, LDEG, 2, LDEG), (2.5 / LDEG), 0.05859375, ((1, 32), (2, 16))),
        "order_of_slot": draw_order_of_slot(jax.random.fold_in(key_list[2], 71), 0),
    }


def legendre_table(orders, colatitude, degrees):
    cosines = jnp.cos(colatitude)
    sine_theta = jnp.sin(colatitude)
    order_float = orders.astype(jnp.float32)[:, None]
    factor_index = jnp.arange(1, degrees, dtype=jnp.int32)
    factor_float = factor_index.astype(jnp.float32)
    log_factors = jnp.log((2.0 * factor_float - 1.0) / (2.0 * factor_float))
    log_product = lax.optimization_barrier(jnp.sum(jnp.where(factor_index[None, :] <= orders[:, None], log_factors[None, :], 0.0), axis=1))
    log_seed = 0.5 * jnp.log((2.0 * order_float + 1.0) / (4.0 * math.pi)) + 0.5 * log_product[:, None] + order_float * jnp.log(sine_theta)[None, :]
    order_square = order_float * order_float
    unit_seed = jnp.ones_like(log_seed)
    rescale_log = 10.0 * math.log(10.0)

    def advance(carry, degree):
        previous, earlier, log_scale = carry
        degree_float = degree.astype(jnp.float32)
        raising = jnp.sqrt(jnp.maximum(4.0 * degree_float * degree_float - 1.0, 1.0) / jnp.maximum(degree_float * degree_float - order_square, 1.0))
        below = degree_float - 1.0
        lowering = jnp.sqrt(jnp.maximum(below * below - order_square, 0.0) / jnp.maximum(4.0 * below * below - 1.0, 1.0))
        recurred = raising * (cosines[None, :] * previous - lowering * earlier)
        current = jnp.where(degree == orders[:, None], unit_seed, jnp.where(degree > orders[:, None], recurred, 0.0))
        large_value = jnp.abs(current) > 10000000000.0
        factor = jnp.where(large_value, 1e-10, 1.0)
        current = current * factor
        previous = previous * factor
        log_scale = log_scale + jnp.where(large_value, rescale_log, 0.0)
        return ((current, previous, log_scale), current * jnp.exp(log_scale))
    blank = jnp.zeros_like(log_seed)
    _, stacked = lax.scan(advance, (blank, blank, log_seed), jnp.arange(degrees, dtype=jnp.int32), unroll=16)
    return stacked

def fourier_table(orders, longitudes):
    product = orders[:, None] * jnp.arange(longitudes, dtype=jnp.int32)[None, :] % longitudes
    angles = 2.0 * math.pi / longitudes * product.astype(jnp.float32)
    weights = jnp.where(orders == 0, 1.0, 2.0).astype(jnp.float32)[:, None]
    return jnp.stack([weights * jnp.cos(angles), -weights * jnp.sin(angles)])

def reference(coefficients, order_of_slot):
    colatitude = math.pi * (jnp.arange(NLAT, dtype=jnp.float32) + 0.5) / NLAT
    legendre = legendre_table(order_of_slot, colatitude, LDEG)
    waves = fourier_table(order_of_slot, NLON)
    padded = jnp.pad(coefficients, ((0, 0), (2, 2), (0, 0), (0, 0), (0, 0)))

    def one_block(block_index):
        start_level = (block_index * R_DEV).astype(jnp.int32)
        window = lax.dynamic_slice_in_dim(padded, start_level, R_DEV + 4, 1).astype(jnp.float32)
        center = window[:, 2:R_DEV + 2]
        slope = (window[:, 0:R_DEV] - 8.0 * window[:, 1:R_DEV + 1] + 8.0 * window[:, 3:R_DEV + 3] - window[:, 4:R_DEV + 4]) / 12.0
        fields = jnp.stack([center, slope], axis=1)
        spectral = jnp.einsum('pqrmcl,lmj->pqrjcm', fields, legendre, precision=lax.Precision.HIGHEST)
        gridded = jnp.einsum('pqrjcm,cmk->pqrjk', spectral, waves, precision=lax.Precision.HIGHEST)
        return gridded.astype(jnp.bfloat16)
    blocks = lax.map(one_block, jnp.arange(N_RAD, dtype=jnp.int32))
    return jnp.moveaxis(blocks, 0, 2).reshape(POT, 2, NR, NLAT, NLON)
```

```python
import math

import jax
import jax.numpy as jnp
from jax import lax
from jax.experimental import pallas as pl
from jax.experimental.pallas import tpu as pltpu
from jax.sharding import PartitionSpec as P

LDEG = 256
NLAT = 384
NLON = 768
HALF = NLON // 2
POT = 4
LEV = 8
SLOTS = 16
PAIRS = 8
ORD = 16
LAT = NLAT // ORD
PITCH = LDEG + 8
ROWS = PAIRS + PAIRS // 2 + 1
LN2 = math.log(2.0)
F32 = jnp.float32
BF16 = jnp.bfloat16


def split(x):
    high = x.astype(BF16)
    return high, (x - high.astype(F32)).astype(BF16)


def legendre_kernel(order_ref, own_ref, halo_ref, out_ref, table, sums):
    first = lax.axis_index("ord") * SLOTS
    slots, orders = [0] * SLOTS, [0] * SLOTS
    for g in range(PAIRS):
        head = order_ref[first + 2 * g]
        odd = head & 1
        even_order = jnp.where(odd == 0, head, LDEG - 1 - head)
        slots[g], slots[PAIRS + g] = 2 * g + odd, 2 * g + 1 - odd
        orders[g], orders[PAIRS + g] = even_order, LDEG - 1 - even_order
    row = lax.broadcasted_iota(jnp.int32, (SLOTS, 128), 0)
    order = jnp.zeros((SLOTS, 128), jnp.int32)
    for i in range(SLOTS):
        order = jnp.where(row == i, orders[i], order)
    m = jnp.concatenate([order, order], axis=1).astype(F32)
    degree = lax.broadcasted_iota(jnp.int32, (SLOTS, LDEG), 1).astype(F32)
    msq = m * m
    raising = jnp.sqrt(jnp.maximum(4.0 * degree * degree - 1.0, 1.0) / jnp.maximum(degree * degree - msq, 1.0))
    below = degree - 1.0
    lowering = jnp.sqrt(jnp.maximum(below * below - msq, 0.0) / jnp.maximum(4.0 * below * below - 1.0, 1.0))
    lowering = raising * lowering
    factor = jnp.maximum(degree, 1.0)
    logs = jnp.log((2.0 * factor - 1.0) / (2.0 * factor))
    logs = jnp.where((degree >= 1.0) & (degree <= m), logs, 0.0)
    product = jnp.sum(logs, axis=1, keepdims=True)
    lat = lax.broadcasted_iota(jnp.int32, (8, NLAT), 1).astype(F32)
    theta = math.pi * (lat + 0.5) / NLAT
    cosine = jnp.cos(theta)
    cosine = jnp.concatenate([cosine, cosine], axis=0)
    log_sine = jnp.log(jnp.sin(theta))
    log_sine = jnp.concatenate([log_sine, log_sine], axis=0)
    m1 = m[:, :1]
    scale = 0.5 * jnp.log((2.0 * m1 + 1.0) / (4.0 * math.pi)) + 0.5 * product + m1 * log_sine

    def block(step, carry):
        last, prior, scale = carry
        start = step * 8
        up = pltpu.roll(raising, LDEG - start, 1)
        down = pltpu.roll(lowering, LDEG - start, 1)
        growth = jnp.exp(scale)
        for j in range(8):
            seed = jnp.where(order == start + j, 1.0, 0.0)
            seed = jnp.concatenate([seed] * 3, axis=1)
            new = (up[:, j:j + 1] * cosine) * last + (seed - down[:, j:j + 1] * prior)
            value = new * growth
            for t in range(3):
                for h in range(2):
                    table[t, pl.ds(h * PAIRS * PITCH + start + j, 8, stride=PITCH), :] = value[8 * h:8 * h + 8, 128 * t:128 * t + 128]
            last, prior = new, last
        large = jnp.abs(last) > 1e10
        shrink = jnp.where(large, 1e-10, 1.0)
        return last * shrink, prior * shrink, scale + jnp.where(large, 10.0 * math.log(10.0), 0.0)

    blank = jnp.zeros((SLOTS, NLAT), F32)
    lax.fori_loop(0, LDEG // 8, block, (blank, blank, scale))

    top = jnp.zeros((8, NLAT), F32)
    for i in range(SLOTS):
        g, eo = i % PAIRS, i // PAIRS
        left = jnp.concatenate([own_ref[slots[i]], halo_ref[slots[i]]], axis=0)
        values = jnp.concatenate([table[t, pl.ds(i * PITCH, LDEG), :] for t in range(3)], axis=1)
        high, low = split(values)
        got = jnp.dot(left, high, preferred_element_type=F32) + jnp.dot(left, low, preferred_element_type=F32)
        top = jnp.maximum(top, jnp.max(jnp.abs(got.reshape(12, 8, NLAT)), axis=0))
        sums[g * 128 + 64 * eo:g * 128 + 64 * eo + 64, :] = got[:64]
        at = (PAIRS + g // 2) * 128 + 64 * (g % 2) + 32 * eo
        sums[at:at + 32, :] = got[64:]
    top = jnp.max(top, axis=0, keepdims=True)
    power = jnp.ceil(jnp.log(jnp.maximum(top, 1e-30)) * (1.0 / LN2) + 0.001) - 15.0
    inverse = jnp.exp(-LN2 * power) * 0.9999
    inverse = jnp.broadcast_to(inverse, (128, NLAT))
    power = jnp.broadcast_to(power, (128, NLAT))
    for k in range(ROWS):
        if k < ROWS - 1:
            coded = jnp.round(sums[k * 128:k * 128 + 128, :] * inverse)
        else:
            coded = power
        coded = jnp.concatenate([coded[:, 128 * t:128 * t + 128].T for t in range(3)], axis=0)
        coded = coded.astype(jnp.int32)
        for d in range(ORD):
            out_ref[d, k] = coded[d * LAT:d * LAT + LAT].astype(jnp.int16)


def fourier_kernel(coded_ref, high_ref, low_ref, out_ref, flat, halo_flat, own, halo):
    p = pl.program_id(0)

    @pl.when(p == 0)
    def _():
        for s in range(ORD):
            unit = jnp.exp(LN2 * coded_ref[s, ROWS - 1].astype(jnp.int32).astype(F32)) * (1.0 / 0.9999)
            for k in range(ROWS - 1):
                value = coded_ref[s, k].astype(jnp.int32).astype(F32) * unit
                if k < PAIRS:
                    at = (s * PAIRS + k) * LAT
                    flat[at:at + LAT, :] = value
                else:
                    at = (s * (PAIRS // 2) + k - PAIRS) * LAT
                    halo_flat[at:at + LAT, :] = value
        for i in range(LAT):
            even = flat[pl.ds(i, 64, stride=2 * LAT), :]
            odd = flat[pl.ds(LAT + i, 64, stride=2 * LAT), :]
            own[pl.ds(i, 128, stride=LAT), :] = jnp.concatenate([even, odd], axis=0).T
            edge = halo_flat[pl.ds(i, 64, stride=LAT), :]
            edge = jnp.concatenate([edge, pltpu.roll(edge, 64, 1)], axis=0).T
            halo[pl.ds(i, 64, stride=LAT), :] = edge[:64]

    def level(eo, c, r):
        if 0 <= r < LEV:
            at = (((eo * POT + p) * LEV + r) * 2 + c) * LAT
            return own[pl.ds(pl.multiple_of(at, 8), LAT), :]
        at = (((eo * POT + p) * 4 + (r + 2 if r < 0 else r - LEV + 2)) * 2 + c) * LAT
        return halo[pl.ds(pl.multiple_of(at, 8), LAT), :]

    totals = []
    for eo in range(2):
        parts = []
        for c in range(2):
            center = [level(eo, c, r) for r in range(-2, LEV + 2)]
            slope = [
                (center[r] - 8.0 * center[r + 1] + 8.0 * center[r + 3] - center[r + 4]) * (1.0 / 12.0)
                for r in range(LEV)
            ]
            parts.append(jnp.concatenate(center[2:-2] + slope, axis=0))
        high, low = split(jnp.concatenate(parts, axis=1))
        wave = high_ref[eo]
        total = jnp.dot(high, wave, preferred_element_type=F32)
        total += jnp.dot(low, wave, preferred_element_type=F32)
        total += jnp.dot(high, low_ref[eo], preferred_element_type=F32)
        totals.append(total)
    both = totals[0] + totals[1]
    out_ref[0, :, :, :, :HALF] = both.astype(BF16).reshape(2, LEV, LAT, HALF)
    both = totals[0] - totals[1]
    out_ref[0, :, :, :, HALF:] = both.astype(BF16).reshape(2, LEV, LAT, HALF)


def waves(order_of_slot):
    pair = order_of_slot.reshape(LDEG // 2, 2)
    even = jnp.where(pair[:, 0] % 2 == 0, pair[:, 0], pair[:, 1])
    even = even.reshape(LDEG // 4, 2).T.reshape(LDEG // 2)
    orders = jnp.stack([even, LDEG - 1 - even])
    product = orders[:, :, None] * jnp.arange(HALF, dtype=jnp.int32) % NLON
    angles = 2.0 * math.pi / NLON * product.astype(F32)
    weights = jnp.where(orders == 0, 1.0, 2.0).astype(F32)[:, :, None]
    table = jnp.concatenate([weights * jnp.cos(angles), -weights * jnp.sin(angles)], axis=1)
    high = lax.reduce_precision(table, 8, 7)
    return high.astype(BF16), (table - high).astype(BF16)


def body(coefficients, order_of_slot):
    count = lax.axis_size("rad")
    head = coefficients[:, :2]
    tail = coefficients[:, LEV - 2:]
    lower = lax.ppermute(tail, "rad", [(i, i + 1) for i in range(count - 1)])
    upper = lax.ppermute(head, "rad", [(i + 1, i) for i in range(count - 1)])
    own = jnp.transpose(coefficients, (2, 0, 1, 3, 4)).reshape(SLOTS, 64, LDEG)
    halo = jnp.concatenate([lower, upper], axis=1)
    halo = jnp.transpose(halo, (2, 0, 1, 3, 4)).reshape(SLOTS, 32, LDEG)
    vmem = pl.BlockSpec(memory_space=pltpu.VMEM)
    coded = pl.pallas_call(
        legendre_kernel,
        out_shape=jax.ShapeDtypeStruct((ORD, ROWS, LAT, 128), jnp.int16),
        in_specs=[pl.BlockSpec(memory_space=pltpu.SMEM), vmem, vmem],
        out_specs=vmem,
        scratch_shapes=[
            pltpu.VMEM((3, SLOTS * PITCH, 128), F32),
            pltpu.VMEM(((ROWS - 1) * 128, NLAT), F32),
        ],
    )(order_of_slot, own, halo)
    coded = lax.all_to_all(coded, "ord", split_axis=0, concat_axis=0, tiled=True)
    high, low = waves(order_of_slot)
    return pl.pallas_call(
        fourier_kernel,
        out_shape=jax.ShapeDtypeStruct((POT, 2, LEV, LAT, NLON), BF16),
        grid=(POT,),
        in_specs=[
            pl.BlockSpec((ORD, ROWS, LAT, 128), lambda p: (0, 0, 0, 0)),
            pl.BlockSpec((2, LDEG, HALF), lambda p: (0, 0, 0)),
            pl.BlockSpec((2, LDEG, HALF), lambda p: (0, 0, 0)),
        ],
        out_specs=pl.BlockSpec((1, 2, LEV, LAT, NLON), lambda p: (p, 0, 0, 0, 0)),
        scratch_shapes=[
            pltpu.VMEM((128 * LAT, 128), F32),
            pltpu.VMEM((64 * LAT, 128), F32),
            pltpu.VMEM((128 * LAT, 128), F32),
            pltpu.VMEM((64 * LAT, 128), F32),
        ],
    )(coded, high, low)


def solution(mesh):
    return jax.shard_map(
        body,
        mesh=mesh,
        in_specs=(P(None, "rad", "ord", None, None), P()),
        out_specs=P(None, None, "rad", "ord", None),
        check_vma=False,
    )
```

```python
import math

import jax
import jax.numpy as jnp
from jax import lax
from jax.experimental import pallas as pl
from jax.experimental.pallas import tpu as pltpu
from jax.sharding import PartitionSpec as P

LDEG = 256
NLAT = 384
NLON = 768
HALF = NLON // 2
POT = 4
LEV = 8
SLOTS = 16
PAIRS = 8
ORD = 16
SIDE = 4
LAT = NLAT // ORD
NORTH = NLAT // 2
ROWS = 9
SCALE_ROW = 2
EDGE = 3
LN2 = math.log(2.0)
F32 = jnp.float32
BF16 = jnp.bfloat16
MESH = pl.DeviceIdType.MESH


def split(x):
    high = x.astype(BF16)
    return high, (x - high.astype(F32)).astype(BF16)


def legendre_kernel(order_ref, own_ref, out_ref, table, sums):
    first = lax.axis_index("ord") * SLOTS
    slots, orders = [0] * SLOTS, [0] * SLOTS
    for g in range(PAIRS):
        head = order_ref[first + 2 * g]
        odd = head & 1
        even_order = jnp.where(odd == 0, head, LDEG - 1 - head)
        slots[g], slots[PAIRS + g] = 2 * g + odd, 2 * g + 1 - odd
        orders[g], orders[PAIRS + g] = even_order, LDEG - 1 - even_order
    row = lax.broadcasted_iota(jnp.int32, (SLOTS, 128), 0)
    order = jnp.zeros((SLOTS, 128), jnp.int32)
    for i in range(SLOTS):
        order = jnp.where(row == i, orders[i], order)
    m = jnp.concatenate([order, order], axis=1).astype(F32)
    degree = lax.broadcasted_iota(jnp.int32, (SLOTS, LDEG), 1).astype(F32)
    msq = m * m
    raising = jnp.sqrt(jnp.maximum(4.0 * degree * degree - 1.0, 1.0) / jnp.maximum(degree * degree - msq, 1.0))
    below = degree - 1.0
    lowering = jnp.sqrt(jnp.maximum(below * below - msq, 0.0) / jnp.maximum(4.0 * below * below - 1.0, 1.0))
    lowering = raising * lowering
    factor = jnp.maximum(degree, 1.0)
    logs = jnp.log((2.0 * factor - 1.0) / (2.0 * factor))
    logs = jnp.where((degree >= 1.0) & (degree <= m), logs, 0.0)
    product = jnp.sum(logs, axis=1, keepdims=True)
    base = 0.5 * jnp.log((2.0 * m[:, :128] + 1.0) / (4.0 * math.pi)) + 0.5 * product

    lane = lax.broadcasted_iota(jnp.int32, (8, 128), 1)
    half = lane < 64

    def tiles(x):
        return [x[:8, :128], x[8:, :128], jnp.where(half, x[:8, :128], x[8:, :128])]

    theta = [math.pi * (lane.astype(F32) + 0.5) / NLAT, math.pi * ((lane & 63).astype(F32) + 128.5) / NLAT]
    cosine = [jnp.cos(t) for t in theta]
    log_sine = [jnp.log(jnp.sin(t)) for t in theta]
    cosine = [cosine[0], cosine[0], cosine[1]]
    log_sine = [log_sine[0], log_sine[0], log_sine[1]]
    order_tiles = tiles(order)
    start_scale = [b + k * s for b, k, s in zip(tiles(base), tiles(m), log_sine)]

    def block(step, carry):
        last, prior, scale = [list(c) for c in carry]
        start = step * 8
        up = pltpu.roll(raising, LDEG - start, 1)
        down = pltpu.roll(lowering, LDEG - start, 1)
        growth = [jnp.exp(s) for s in scale]
        for j in range(8):
            at = pl.multiple_of((start + j) * 8, 8)
            ups = tiles(jnp.broadcast_to(up[:, j:j + 1], (SLOTS, 128)))
            downs = tiles(jnp.broadcast_to(down[:, j:j + 1], (SLOTS, 128)))
            for t in range(3):
                seed = jnp.where(order_tiles[t] == start + j, 1.0, 0.0)
                new = (ups[t] * cosine[t]) * last[t] + (seed - downs[t] * prior[t])
                table[t, pl.ds(at, 8), :] = new * growth[t]
                last[t], prior[t] = new, last[t]
        for t in range(3):
            large = jnp.abs(last[t]) > 1e10
            shrink = jnp.where(large, 1e-10, 1.0)
            last[t], prior[t] = last[t] * shrink, prior[t] * shrink
            scale[t] = scale[t] + jnp.where(large, 10.0 * math.log(10.0), 0.0)
        return tuple(last), tuple(prior), tuple(scale)

    blank = tuple(jnp.zeros((8, 128), F32) for _ in range(3))
    lax.fori_loop(0, LDEG // 8, block, (blank, blank, tuple(start_scale)))

    parity = lax.broadcasted_iota(jnp.int32, (64, LDEG), 1) & 1
    parity = parity.astype(F32).astype(BF16)
    wide = lax.broadcasted_iota(jnp.int32, (64, 128), 1) < 64
    top = [jnp.zeros((8, 128), F32) for _ in range(3)]
    for g in range(PAIRS):
        shared = table[2, pl.ds(g, LDEG, stride=8), :]
        for eo in range(2):
            left = own_ref[slots[eo * PAIRS + g]]
            odd_left = left * parity
            left = jnp.concatenate([left - odd_left, odd_left], axis=0)
            values = jnp.concatenate([table[eo, pl.ds(g, LDEG, stride=8), :], shared], axis=1)
            right = jnp.concatenate(split(values), axis=0)
            got = jnp.dot(jnp.concatenate([left, left], axis=1), right, preferred_element_type=F32)
            north = got[:64] + got[64:]
            south = got[:64] - got[64:] if eo == 0 else got[64:] - got[:64]
            near, far = north[:, 128:], south[:, 128:]
            if eo == 0:
                mixed = jnp.where(wide, near, pltpu.roll(far, 64, 1))
            else:
                mixed = jnp.where(wide, pltpu.roll(near, 64, 1), far)
            at = (2 * g + eo) * 64
            for t, part in enumerate((north[:, :128], south[:, :128], mixed)):
                sums[t, at:at + 64, :] = part
                top[t] = jnp.maximum(top[t], jnp.max(jnp.abs(part.reshape(8, 8, 128)), axis=0))

    for t in range(3):
        peak = jnp.max(top[t], axis=0, keepdims=True)
        power = jnp.ceil(jnp.log(jnp.maximum(peak, 1e-30)) * (1.0 / LN2) + 0.001) - 15.0
        inverse = jnp.broadcast_to(jnp.exp(-LN2 * power) * 0.9999, (128, 128))
        for k in range(ROWS):
            if k == SCALE_ROW:
                coded = jnp.broadcast_to(power, (128, 128))
            else:
                pieces = []
                if k < SCALE_ROW:
                    picks = [(2 * q + k, eo, r) for q in range(4) for eo in range(2) for r in (0, 1)]
                elif k < SCALE_ROW + EDGE:
                    picks = [(2 * q + k - EDGE, eo, r) for q in range(4) for eo in range(2) for r in (6, 7)]
                else:
                    picks = [(4 * h + k - 5, eo, r) for h in range(2) for eo in range(2) for r in (2, 3, 4, 5)]
                for g, eo, r in picks:
                    pieces.append(sums[t, pl.ds((2 * g + eo) * 64 + r, 8, stride=8), :])
                coded = jnp.round(jnp.concatenate(pieces, axis=0) * inverse)
            coded = coded.T.astype(jnp.int32)
            if t < 2:
                spans = [(d, 0, LAT, LAT * d) for d in range(5)] + [(5, 0, 8, 120)]
                spans = [(d if t == 0 else ORD - 1 - d, lo, hi, at) for d, lo, hi, at in spans]
            else:
                spans = [(5, 8, LAT, 0), (6, 0, LAT, 16), (7, 0, LAT, 40)]
                spans = spans + [(ORD - 1 - d, lo, hi, at + 64) for d, lo, hi, at in spans]
            for d, lo, hi, at in spans:
                out_ref[d, k, lo:hi, :] = coded[at:at + hi - lo].astype(jnp.int16)


def turn(product):
    rest = product - NLON * jnp.floor(product * (1.0 / NLON))
    quarter = jnp.floor(rest * (1.0 / 192.0) + 0.5)
    x = (rest - 192.0 * quarter) * (2.0 * math.pi / NLON)
    y = x * x
    sine = x * (1.0 + y * (-1.0 / 6.0 + y * (1.0 / 120.0 + y * (-1.0 / 5040.0 + y * (1.0 / 362880.0)))))
    cosine = 1.0 + y * (-0.5 + y * (1.0 / 24.0 + y * (-1.0 / 720.0 + y * (1.0 / 40320.0 - y * (1.0 / 3628800.0)))))
    swap = (quarter == 1.0) | (quarter == 3.0)
    first = jnp.where(swap, sine, cosine)
    second = jnp.where(swap, cosine, sine)
    first = jnp.where((quarter == 1.0) | (quarter == 2.0), -first, first)
    second = jnp.where((quarter == 2.0) | (quarter == 3.0), -second, second)
    return first, second


def wave_tables(order_ref, main_ref, tail_ref):
    row = lax.broadcasted_iota(jnp.int32, (128, LDEG), 0)
    lane = lax.broadcasted_iota(jnp.int32, (128, LDEG), 1)
    source = (row & 15) * SLOTS + 2 * (row >> 4)
    heads = jnp.broadcast_to(order_ref[...], (128, LDEG)).astype(F32)
    head = jnp.sum(jnp.where(lane == source, heads, 0.0), axis=1, keepdims=True)
    even = jnp.where(head - 2.0 * jnp.floor(0.5 * head) == 0.0, head, LDEG - 1 - head)
    for eo in range(2):
        order = jnp.broadcast_to(even if eo == 0 else LDEG - 1 - even, (128, 128))
        weight = jnp.where(order == 0.0, 1.0, 2.0)
        for j in range(3):
            k = lax.broadcasted_iota(jnp.int32, (128, 128), 1).astype(F32) + 128.0 * j
            cosine, sine = turn(order * k)
            for c, wave in enumerate((weight * cosine, -weight * sine)):
                high, low = split(wave)
                at = c * 128
                if j < 2:
                    columns = pl.ds(128 * j, 128)
                    main_ref[eo, at:at + 128, columns] = high
                    main_ref[eo, LDEG + at:LDEG + at + 128, columns] = high
                    main_ref[eo, 2 * LDEG + at:2 * LDEG + at + 128, columns] = low
                else:
                    for b in range(2):
                        tail_ref[eo, b * LDEG + at:b * LDEG + at + 128, :128] = high
                        tail_ref[eo, b * LDEG + at:b * LDEG + at + 128, 128:] = low


OFFSETS = [(dy, dx) for dy in range(SIDE) for dx in range(SIDE) if (dy, dx) != (0, 0)]


def exchange_kernel(order_ref, coded_ref, got_ref, edge_ref, main_ref, tail_ref, own_sem, send_sem, recv_sem, up_send, up_recv, down_send, down_recv):
    me = lax.axis_index("ord")
    y, x = me // SIDE, me % SIDE
    rad = lax.axis_index("rad")
    count = lax.axis_size("rad")
    upper, lower = (rad + 1) % count, (rad + count - 1) % count

    def other(dy, dx):
        return (y + dy) % SIDE * SIDE + (x + dx) % SIDE

    barrier = pltpu.get_barrier_semaphore()
    for dy, dx in OFFSETS:
        pl.semaphore_signal(barrier, inc=1, device_id={"ord": other(dy, dx)}, device_id_type=MESH)
    for neighbour in (lower, upper):
        pl.semaphore_signal(barrier, inc=1, device_id={"rad": neighbour}, device_id_type=MESH)
    pl.semaphore_wait(barrier, len(OFFSETS) + 2)

    sends = []
    for n, (dy, dx) in enumerate(OFFSETS):
        peer = other(dy, dx)
        copy = pltpu.make_async_remote_copy(
            src_ref=coded_ref.at[peer], dst_ref=got_ref.at[me], send_sem=send_sem.at[n], recv_sem=recv_sem.at[n],
            device_id={"ord": peer}, device_id_type=MESH,
        )
        copy.start()
        sends.append(copy)
    own = pltpu.make_async_copy(coded_ref.at[me], got_ref.at[me], own_sem)
    own.start()
    passed = []

    def pass_on(block, source, n):
        down = pltpu.make_async_remote_copy(
            src_ref=block.at[0:EDGE], dst_ref=edge_ref.at[1, source], send_sem=down_send.at[n], recv_sem=down_recv.at[n],
            device_id={"rad": lower}, device_id_type=MESH,
        )
        up = pltpu.make_async_remote_copy(
            src_ref=block.at[SCALE_ROW:SCALE_ROW + EDGE], dst_ref=edge_ref.at[0, source], send_sem=up_send.at[n], recv_sem=up_recv.at[n],
            device_id={"rad": upper}, device_id_type=MESH,
        )
        down.start()
        up.start()
        passed.extend([down, up])

    pass_on(coded_ref.at[me], me, len(OFFSETS))
    wave_tables(order_ref, main_ref, tail_ref)
    for n, (dy, dx) in enumerate(OFFSETS):
        sends[n].wait_recv()
        source = other(SIDE - dy, SIDE - dx)
        pass_on(got_ref.at[source], source, n)
    own.wait()
    for copy in sends:
        copy.wait_send()
    for copy in passed:
        copy.wait()


def fourier_kernel(got_ref, edge_ref, main_ref, tail_ref, out_ref, middle, edges, inner, outer):
    p = pl.program_id(0)

    @pl.when(p == 0)
    def _():
        rad = lax.axis_index("rad")
        count = lax.axis_size("rad")
        keep_low = jnp.where(rad == 0, 0.0, 1.0) * (1.0 / 0.9999)
        keep_high = jnp.where(rad == count - 1, 0.0, 1.0) * (1.0 / 0.9999)

        def value(coded):
            return coded.astype(jnp.int32).astype(F32)

        for s in range(ORD):
            unit = jnp.exp(LN2 * value(got_ref[s, SCALE_ROW])) * (1.0 / 0.9999)
            for k in range(4):
                at = (k * ORD + s) * LAT
                middle[at:at + LAT, :] = value(got_ref[s, 5 + k]) * unit
            below = jnp.exp(LN2 * value(edge_ref[0, s, 0])) * keep_low
            above = jnp.exp(LN2 * value(edge_ref[1, s, SCALE_ROW])) * keep_high
            for k in range(2):
                at = (k * ORD + s) * LAT
                edges[0, at:at + LAT, :] = value(got_ref[s, k]) * unit
                edges[1, at:at + LAT, :] = value(got_ref[s, EDGE + k]) * unit
                edges[2, at:at + LAT, :] = value(edge_ref[0, s, 1 + k]) * below
                edges[3, at:at + LAT, :] = value(edge_ref[1, s, k]) * above
        mirror = lax.axis_index("ord") >= ORD // 2
        lane = lax.broadcasted_iota(jnp.int32, (32, 128), 1)

        def one(i, _):
            at = jnp.where(mirror, LAT - 1 - i, i)
            mid = middle[pl.ds(at, 64, stride=LAT), :]
            mid = jnp.concatenate([mid, pltpu.roll(mid, 64, 1)], axis=0)
            parts = [edges[e, pl.ds(at, 32, stride=LAT), :] for e in range(4)]
            near, far = [], []
            for q in range(4):
                def shifted(e, place):
                    amount = (place - 32 * q) % 128
                    return pltpu.roll(parts[e], amount, 1) if amount else parts[e]
                near.append(jnp.where(lane < 64, mid[32 * q:32 * q + 32], jnp.where(lane < 96, shifted(0, 64), shifted(1, 96))))
                far.append(jnp.where(lane < 32, shifted(2, 0), shifted(3, 32)))
            inner[pl.ds(i, 128, stride=LAT), :] = jnp.concatenate(near, axis=0).T
            outer[pl.ds(i, 64, stride=LAT), :] = jnp.concatenate(far, axis=0).T[:64]
            return 0

        lax.fori_loop(0, LAT, one, 0)

    def level(eo, c, r):
        tail = 2 * p + c
        if r < 0:
            ref, at = outer, eo * 16 + (r + 2) * 8
        elif r < 2:
            ref, at = inner, 64 + eo * 16 + r * 8
        elif r < 6:
            ref, at = inner, eo * 32 + (r - 2) * 8
        elif r < 8:
            ref, at = inner, 96 + eo * 16 + (r - 6) * 8
        else:
            ref, at = outer, 32 + eo * 16 + (r - 8) * 8
        return ref[pl.ds(pl.multiple_of((at + tail) * LAT, 8), LAT), :]

    totals = []
    for eo in range(2):
        parts = [jnp.concatenate([level(eo, c, r) for r in range(-2, LEV + 2)], axis=0) for c in range(2)]
        high, low = split(jnp.concatenate(parts, axis=1))
        main = jnp.dot(jnp.concatenate([high, low, high], axis=1), main_ref[eo], preferred_element_type=F32)
        tail = jnp.dot(jnp.concatenate([high, low], axis=1), tail_ref[eo], preferred_element_type=F32)
        totals.append(jnp.concatenate([main, tail[:, :128] + tail[:, 128:]], axis=1))
    for side in range(2):
        total = totals[0] + totals[1] if side == 0 else totals[0] - totals[1]
        columns = pl.ds(side * HALF, HALF)
        for r in range(LEV):
            level_of = [total[(r + d) * LAT:(r + d + 1) * LAT] for d in range(5)]
            out_ref[0, 0, r, :, columns] = level_of[2].astype(BF16)
            slope = (level_of[0] - level_of[4]) * (1.0 / 12.0) + (level_of[3] - level_of[1]) * (8.0 / 12.0)
            out_ref[0, 1, r, :, columns] = slope.astype(BF16)


def body(coefficients, order_of_slot):
    own = jnp.transpose(coefficients, (2, 0, 3, 1, 4)).reshape(SLOTS, 64, LDEG)
    vmem = pl.BlockSpec(memory_space=pltpu.VMEM)
    anywhere = pl.BlockSpec(memory_space=pl.ANY)
    coded = pl.pallas_call(
        legendre_kernel,
        out_shape=jax.ShapeDtypeStruct((ORD, ROWS, LAT, 128), jnp.int16),
        in_specs=[pl.BlockSpec(memory_space=pltpu.SMEM), vmem],
        out_specs=vmem,
        scratch_shapes=[
            pltpu.VMEM((3, LDEG * 8, 128), F32),
            pltpu.VMEM((3, SLOTS * 64, 128), F32),
        ],
    )(order_of_slot, own)
    peers = len(OFFSETS)
    got, edge, main, tail = pl.pallas_call(
        exchange_kernel,
        out_shape=[
            jax.ShapeDtypeStruct((ORD, ROWS, LAT, 128), jnp.int16),
            jax.ShapeDtypeStruct((2, ORD, EDGE, LAT, 128), jnp.int16),
            jax.ShapeDtypeStruct((2, 3 * LDEG, 256), BF16),
            jax.ShapeDtypeStruct((2, 2 * LDEG, 256), BF16),
        ],
        in_specs=[vmem, anywhere],
        out_specs=[anywhere, anywhere, vmem, vmem],
        scratch_shapes=[
            pltpu.SemaphoreType.DMA,
            pltpu.SemaphoreType.DMA((peers,)),
            pltpu.SemaphoreType.DMA((peers,)),
            pltpu.SemaphoreType.DMA((ORD,)),
            pltpu.SemaphoreType.DMA((ORD,)),
            pltpu.SemaphoreType.DMA((ORD,)),
            pltpu.SemaphoreType.DMA((ORD,)),
        ],
        compiler_params=pltpu.CompilerParams(collective_id=0, has_side_effects=True),
    )(order_of_slot.reshape(1, LDEG), coded)
    return pl.pallas_call(
        fourier_kernel,
        out_shape=jax.ShapeDtypeStruct((POT, 2, LEV, LAT, NLON), BF16),
        grid=(POT,),
        in_specs=[
            pl.BlockSpec((ORD, ROWS, LAT, 128), lambda p: (0, 0, 0, 0)),
            pl.BlockSpec((2, ORD, EDGE, LAT, 128), lambda p: (0, 0, 0, 0, 0)),
            pl.BlockSpec((2, 3 * LDEG, 256), lambda p: (0, 0, 0)),
            pl.BlockSpec((2, 2 * LDEG, 256), lambda p: (0, 0, 0)),
        ],
        out_specs=pl.BlockSpec((1, 2, LEV, LAT, NLON), lambda p: (p, 0, 0, 0, 0)),
        scratch_shapes=[
            pltpu.VMEM((64 * LAT, 128), F32),
            pltpu.VMEM((4, 32 * LAT, 128), F32),
            pltpu.VMEM((128 * LAT, 128), F32),
            pltpu.VMEM((64 * LAT, 128), F32),
        ],
    )(got, edge, main, tail)


def solution(mesh):
    return jax.shard_map(
        body,
        mesh=mesh,
        in_specs=(P(None, "rad", "ord", None, None), P()),
        out_specs=P(None, None, "rad", "ord", None),
        check_vma=False,
    )
```

```python
import math

import jax
import jax.numpy as jnp
from jax import lax
from jax.experimental import pallas as pl
from jax.experimental.pallas import tpu as pltpu
from jax.sharding import PartitionSpec as P

LDEG = 256
NLAT = 384
NLON = 768
HALF = NLON // 2
POT = 4
LEV = 8
SLOTS = 16
PAIRS = 8
ORD = 16
SIDE = 4
LAT = NLAT // ORD
NORTH = NLAT // 2
UNITS = 25
SCALE = 6
EDGE = 7
FIRST = (0, 3, 7, 10, 13, 16, 19, 22)
STEP = 32
GROUP = 6
LOOP = True
LN2 = math.log(2.0)
F32 = jnp.float32
BF16 = jnp.bfloat16
MESH = pl.DeviceIdType.MESH


def split(x):
    high = x.astype(BF16)
    return high, (x - high.astype(F32)).astype(BF16)


def legendre(order_ref, own_ref, ready_copies, out_ref, fresh, spare, high_table, low_table, sums):
    first = lax.axis_index("ord") * SLOTS
    slots, orders = [0] * SLOTS, [0] * SLOTS
    for g in range(PAIRS):
        head = order_ref[first + 2 * g]
        odd = head & 1
        even_order = jnp.where(odd == 0, head, LDEG - 1 - head)
        slots[g], slots[PAIRS + g] = 2 * g + odd, 2 * g + 1 - odd
        orders[g], orders[PAIRS + g] = even_order, LDEG - 1 - even_order
    row = lax.broadcasted_iota(jnp.int32, (SLOTS, 128), 0)
    order = jnp.zeros((SLOTS, 128), jnp.int32)
    for i in range(SLOTS):
        order = jnp.where(row == i, orders[i], order)
    m = jnp.concatenate([order, order], axis=1).astype(F32)
    degree = lax.broadcasted_iota(jnp.int32, (SLOTS, LDEG), 1).astype(F32)
    msq = m * m
    raising = jnp.sqrt(jnp.maximum(4.0 * degree * degree - 1.0, 1.0) / jnp.maximum(degree * degree - msq, 1.0))
    below = degree - 1.0
    lowering = jnp.sqrt(jnp.maximum(below * below - msq, 0.0) / jnp.maximum(4.0 * below * below - 1.0, 1.0))
    lowering = raising * lowering
    factor = jnp.maximum(degree, 1.0)
    logs = jnp.log((2.0 * factor - 1.0) / (2.0 * factor))
    logs = jnp.where((degree >= 1.0) & (degree <= m), logs, 0.0)
    product = jnp.sum(logs, axis=1, keepdims=True)
    base = 0.5 * jnp.log((2.0 * m[:, :128] + 1.0) / (4.0 * math.pi)) + 0.5 * product

    lane = lax.broadcasted_iota(jnp.int32, (8, 128), 1)
    half = lane < 64

    def tiles(x):
        return [x[:8, :128], x[8:, :128], jnp.where(half, x[:8, :128], x[8:, :128])]

    theta = [math.pi * (lane.astype(F32) + 0.5) / NLAT, math.pi * ((lane & 63).astype(F32) + 128.5) / NLAT]
    cosine = [jnp.cos(t) for t in theta]
    log_sine = [jnp.log(jnp.sin(t)) for t in theta]
    cosine = [cosine[0], cosine[0], cosine[1]]
    log_sine = [log_sine[0], log_sine[0], log_sine[1]]
    order_tiles = tiles(order)
    start_scale = [b + k * s for b, k, s in zip(tiles(base), tiles(m), log_sine)]

    spare[...] = jnp.zeros_like(spare)

    def refine(stage, t, s, at):
        values = stage[t, pl.ds(s, STEP, stride=8), :]
        high, low = split(values)
        high_table[t, s, pl.ds(at, STEP), :] = high
        low_table[t, s, pl.ds(at, STEP), :] = low

    def block(step, carry):
        last, prior, scale = [list(c) for c in carry]
        for side, (stage, ready) in enumerate(((fresh, spare), (spare, fresh))):
            start = (2 * step + side) * STEP
            at = pl.multiple_of(start, STEP)
            up = pltpu.roll(raising, LDEG - start, 1)
            down = pltpu.roll(lowering, LDEG - start, 1)
            jobs = [(t, s) for t in range(3) for s in range(PAIRS)]
            for j in range(STEP):
                if j % 8 == 0:
                    growth = [jnp.exp(s) for s in scale]
                ups = tiles(jnp.broadcast_to(up[:, j:j + 1], (SLOTS, 128)))
                downs = tiles(jnp.broadcast_to(down[:, j:j + 1], (SLOTS, 128)))
                for t in range(3):
                    seed = jnp.where(order_tiles[t] == start + j, 1.0, 0.0)
                    new = (ups[t] * cosine[t]) * last[t] + (seed - downs[t] * prior[t])
                    stage[t, 8 * j:8 * j + 8, :] = new * growth[t]
                    last[t], prior[t] = new, last[t]
                if j % 8 == 7:
                    for t in range(3):
                        large = jnp.abs(last[t]) > 1e10
                        shrink = jnp.where(large, 1e-10, 1.0)
                        last[t], prior[t] = last[t] * shrink, prior[t] * shrink
                        scale[t] = scale[t] + jnp.where(large, 10.0 * math.log(10.0), 0.0)
                while jobs and len(jobs) * STEP > 24 * (STEP - 1 - j):
                    t, s = jobs.pop()
                    refine(ready, t, s, at)
        return tuple(last), tuple(prior), tuple(scale)

    blank = tuple(jnp.zeros((8, 128), F32) for _ in range(3))
    lax.fori_loop(0, LDEG // (2 * STEP), block, (blank, blank, tuple(start_scale)))
    for t in range(3):
        for s in range(PAIRS):
            refine(spare, t, s, LDEG)

    parity = lax.broadcasted_iota(jnp.int32, (64, LDEG), 1) & 1
    parity = parity.astype(F32).astype(BF16)
    wide = lax.broadcasted_iota(jnp.int32, (64, 128), 1) < 64
    for copy in ready_copies:
        copy.wait()
    top = [jnp.zeros((8, 128), F32) for _ in range(3)]
    body_rows = slice(STEP, STEP + LDEG)
    for g in range(PAIRS):
        for eo in range(2):
            left = own_ref[slots[eo * PAIRS + g]].reshape(64, LDEG)
            odd_left = left * parity
            left = jnp.concatenate([left - odd_left, odd_left], axis=0)
            right = jnp.concatenate(
                [jnp.concatenate([table[eo, g, body_rows], table[2, g, body_rows]], axis=1) for table in (high_table, low_table)],
                axis=0,
            )
            got = jnp.dot(jnp.concatenate([left, left], axis=1), right, preferred_element_type=F32)
            north = got[:64] + got[64:]
            south = got[:64] - got[64:] if eo == 0 else got[64:] - got[:64]
            near, far = north[:, 128:], south[:, 128:]
            if eo == 0:
                mixed = jnp.where(wide, near, pltpu.roll(far, 64, 1))
            else:
                mixed = jnp.where(wide, pltpu.roll(near, 64, 1), far)
            at = (2 * g + eo) * 64
            for t, part in enumerate((north[:, :128], south[:, :128], mixed)):
                sums[t, at:at + 64, :] = part
                top[t] = jnp.maximum(top[t], jnp.max(jnp.abs(part.reshape(8, 8, 128)), axis=0))

    powers = []
    for t in range(3):
        peak = jnp.max(top[t], axis=0, keepdims=True)
        power = jnp.ceil(jnp.log(jnp.maximum(peak, 1e-30)) * (1.0 / LN2) + 0.001) - 15.0
        inverse = jnp.broadcast_to(jnp.exp(-LN2 * power) * 0.9999, (128, 128))
        powers.append(power)
        for k in range(8):
            if k < 2:
                picks = [(2 * q + k, eo, r) for q in range(4) for eo in range(2) for r in (0, 1)]
            elif k < 4:
                picks = [(2 * q + k - 2, eo, r) for q in range(4) for eo in range(2) for r in (6, 7)]
            else:
                picks = [(4 * h + k - 4, eo, r) for h in range(2) for eo in range(2) for r in (2, 3, 4, 5)]
            pieces = [sums[t, (2 * g + eo) * 64 + 8 * r:(2 * g + eo) * 64 + 8 * r + 8, :] for g, eo, r in picks]
            coded = jnp.round(jnp.concatenate(pieces, axis=0) * inverse)
            coded = coded.T.astype(jnp.int32)
            if t < 2:
                spans = [(d, 0, 3, LAT * d) for d in range(5)] + [(5, 0, 1, 120)]
                spans = [(d if t == 0 else ORD - 1 - d, lo, hi, at) for d, lo, hi, at in spans]
            else:
                spans = [(5, 1, 3, 0), (6, 0, 3, 16), (7, 0, 3, 40)]
                spans = spans + [(ORD - 1 - d, lo, hi, at + 64) for d, lo, hi, at in spans]
            for d, lo, hi, at in spans:
                part = coded[at:at + 8 * (hi - lo)].reshape(hi - lo, 8, 128)
                out_ref[d, FIRST[k] + lo:FIRST[k] + hi] = part.astype(jnp.int16)
    sublane = lax.broadcasted_iota(jnp.int32, (8, 128), 0)
    power = jnp.where(sublane == 0, powers[0], jnp.where(sublane == 1, powers[1], powers[2]))
    power = power.astype(jnp.int32).astype(jnp.int16)
    for d in range(ORD):
        out_ref[d, SCALE] = power


def turn(product):
    rest = product - NLON * jnp.floor(product * (1.0 / NLON))
    quarter = jnp.floor(rest * (1.0 / 192.0) + 0.5)
    x = (rest - 192.0 * quarter) * (2.0 * math.pi / NLON)
    y = x * x
    sine = x * (1.0 + y * (-1.0 / 6.0 + y * (1.0 / 120.0 + y * (-1.0 / 5040.0 + y * (1.0 / 362880.0)))))
    cosine = 1.0 + y * (-0.5 + y * (1.0 / 24.0 + y * (-1.0 / 720.0 + y * (1.0 / 40320.0 - y * (1.0 / 3628800.0)))))
    swap = (quarter == 1.0) | (quarter == 3.0)
    first = jnp.where(swap, sine, cosine)
    second = jnp.where(swap, cosine, sine)
    first = jnp.where((quarter == 1.0) | (quarter == 2.0), -first, first)
    second = jnp.where((quarter == 2.0) | (quarter == 3.0), -second, second)
    return first, second


def wave_tables(order_ref, main_ref, tail_ref):
    row = lax.broadcasted_iota(jnp.int32, (128, LDEG), 0)
    lane = lax.broadcasted_iota(jnp.int32, (128, LDEG), 1)
    source = (row & 15) * SLOTS + 2 * (row >> 4)
    heads = jnp.broadcast_to(order_ref[...], (128, LDEG)).astype(F32)
    head = jnp.sum(jnp.where(lane == source, heads, 0.0), axis=1, keepdims=True)
    even = jnp.where(head - 2.0 * jnp.floor(0.5 * head) == 0.0, head, LDEG - 1 - head)
    for eo in range(2):
        order = jnp.broadcast_to(even if eo == 0 else LDEG - 1 - even, (128, 128))
        weight = jnp.where(order == 0.0, 1.0, 2.0)
        for j in range(3):
            k = lax.broadcasted_iota(jnp.int32, (128, 128), 1).astype(F32) + 128.0 * j
            cosine, sine = turn(order * k)
            for c, wave in enumerate((weight * cosine, -weight * sine)):
                high, low = split(wave)
                at = c * 128
                if j < 2:
                    columns = pl.ds(128 * j, 128)
                    main_ref[eo, at:at + 128, columns] = high
                    main_ref[eo, LDEG + at:LDEG + at + 128, columns] = high
                    main_ref[eo, 2 * LDEG + at:2 * LDEG + at + 128, columns] = low
                else:
                    for b in range(2):
                        tail_ref[eo, b * LDEG + at:b * LDEG + at + 128, :128] = high
                        tail_ref[eo, b * LDEG + at:b * LDEG + at + 128, 128:] = low


OFFSETS = [(dy, dx) for dy in range(SIDE) for dx in range(SIDE) if (dy, dx) != (0, 0)]
OFFSETS.sort(key=lambda o: -min(o[0], SIDE - o[0]) - min(o[1], SIDE - o[1]))


def exchange_kernel(
    order_ref, heads_ref, coefficients_ref, got_ref, edge_ref, main_ref, tail_ref,
    own_ref, coded_ref, fresh, spare, high_table, low_table, sums,
    load_sem, own_sem, send_sem, recv_sem, up_send, up_recv, down_send, down_recv,
):
    me = lax.axis_index("ord")
    y, x = me // SIDE, me % SIDE
    rad = lax.axis_index("rad")
    count = lax.axis_size("rad")
    upper, lower = (rad + 1) % count, (rad + count - 1) % count

    def other(dy, dx):
        return (y + dy) % SIDE * SIDE + (x + dx) % SIDE

    barrier = pltpu.get_barrier_semaphore()
    for dy, dx in OFFSETS:
        pl.semaphore_signal(barrier, inc=1, device_id={"ord": other(dy, dx)}, device_id_type=MESH)
    for neighbour in (lower, upper):
        pl.semaphore_signal(barrier, inc=1, device_id={"rad": neighbour}, device_id_type=MESH)

    loads = []
    for p in range(POT):
        for r in range(LEV):
            copy = pltpu.make_async_copy(coefficients_ref.at[p, r], own_ref.at[:, r, p], load_sem.at[p * LEV + r])
            copy.start()
            loads.append(copy)
    legendre(order_ref, own_ref, loads, coded_ref, fresh, spare, high_table, low_table, sums)
    pl.semaphore_wait(barrier, len(OFFSETS) + 2)

    sends = []
    for n, (dy, dx) in enumerate(OFFSETS):
        peer = other(dy, dx)
        copy = pltpu.make_async_remote_copy(
            src_ref=coded_ref.at[peer], dst_ref=got_ref.at[me], send_sem=send_sem.at[n], recv_sem=recv_sem.at[n],
            device_id={"ord": peer}, device_id_type=MESH,
        )
        copy.start()
        sends.append(copy)
    own = pltpu.make_async_copy(coded_ref.at[me], got_ref.at[me], own_sem)
    own.start()
    passed = []

    def pass_on(block, source, n):
        down = pltpu.make_async_remote_copy(
            src_ref=block.at[0:EDGE], dst_ref=edge_ref.at[1, source], send_sem=down_send.at[n], recv_sem=down_recv.at[n],
            device_id={"rad": lower}, device_id_type=MESH,
        )
        up = pltpu.make_async_remote_copy(
            src_ref=block.at[SCALE:SCALE + EDGE], dst_ref=edge_ref.at[0, source], send_sem=up_send.at[n], recv_sem=up_recv.at[n],
            device_id={"rad": upper}, device_id_type=MESH,
        )
        down.start()
        up.start()
        passed.extend([down, up])

    pass_on(coded_ref.at[me], me, len(OFFSETS))
    wave_tables(heads_ref, main_ref, tail_ref)
    for n, (dy, dx) in enumerate(OFFSETS):
        sends[n].wait_recv()
        source = other(SIDE - dy, SIDE - dx)
        pass_on(got_ref.at[source], source, n)
    own.wait()
    for copy in sends:
        copy.wait_send()
    for copy in passed:
        copy.wait()


def fourier_kernel(got_ref, edge_ref, main_ref, tail_ref, out_ref, middle, edges, scales, turned, inner, outer, result, sem):
    rad = lax.axis_index("rad")
    count = lax.axis_size("rad")
    keep_low = jnp.where(rad == 0, 0.0, 1.0) * (1.0 / 0.9999)
    keep_high = jnp.where(rad == count - 1, 0.0, 1.0) * (1.0 / 0.9999)
    place = lax.axis_index("ord")
    mirror = place >= ORD // 2
    first = jnp.where(mirror, ORD - 1 - place, place) * LAT

    def value(coded):
        return coded.astype(jnp.int32).astype(F32)

    def take(coded):
        return value(coded).reshape(LAT, 128)

    for s in range(ORD):
        for k in range(4):
            at = (k * ORD + s) * LAT
            middle[at:at + LAT, :] = take(got_ref[s, 13 + 3 * k:16 + 3 * k])
        for k in range(2):
            at = (k * ORD + s) * LAT
            edges[0, at:at + LAT, :] = take(got_ref[s, 3 * k:3 * k + 3])
            edges[1, at:at + LAT, :] = take(got_ref[s, 7 + 3 * k:10 + 3 * k])
            edges[2, at:at + LAT, :] = take(edge_ref[0, s, 1 + 3 * k:4 + 3 * k])
            edges[3, at:at + LAT, :] = take(edge_ref[1, s, 3 * k:3 * k + 3])
        scales[0, 8 * s:8 * s + 8, :] = value(got_ref[s, SCALE])
        scales[1, 8 * s:8 * s + 8, :] = value(edge_ref[0, s, 0])
        scales[2, 8 * s:8 * s + 8, :] = value(edge_ref[1, s, SCALE])
    for e in range(3):
        for t in range(3):
            row = scales[e, pl.ds(t, ORD, stride=8), :]
            turned[e, 128 * t:128 * t + 128, :] = jnp.concatenate([row] * 8, axis=0).T

    lane = lax.broadcasted_iota(jnp.int32, (32, 128), 1)

    def one(i):
        at = jnp.where(mirror, LAT - 1 - i, i)
        north = first + at
        row = jnp.where(north < 128, north + jnp.where(mirror, 128, 0), north + 128 + jnp.where(mirror, 64, 0))
        unit = [jnp.exp(LN2 * turned[e, pl.ds(row, 1), :]) for e in range(3)]
        mid = middle[pl.ds(at, 64, stride=LAT), :]
        mid = jnp.concatenate([mid, pltpu.roll(mid, 64, 1)], axis=0)
        parts = [edges[e, pl.ds(at, 32, stride=LAT), :] for e in range(4)]
        near, far = [], []
        for q in range(4):
            def shifted(e, target):
                amount = (target - 32 * q) % 128
                return pltpu.roll(parts[e], amount, 1) if amount else parts[e]
            near.append(jnp.where(lane < 64, mid[32 * q:32 * q + 32], jnp.where(lane < 96, shifted(0, 64), shifted(1, 96))))
            far.append(jnp.where(lane < 32, shifted(2, 0), shifted(3, 32)))
        far = jnp.concatenate(far, axis=0).T
        inner[pl.ds(i, 128, stride=LAT), :] = jnp.concatenate(near, axis=0).T * (unit[0] * (1.0 / 0.9999))
        outer[pl.ds(i, 32, stride=LAT), :] = far[:32] * (unit[1] * keep_low)
        outer[pl.ds(32 * LAT + i, 32, stride=LAT), :] = far[32:64] * (unit[2] * keep_high)

    @pl.loop(0, LAT // GROUP)
    def _(n):
        for i in range(GROUP):
            one(n * GROUP + i)

    def level(eo, c, p, r):
        tail = 2 * p + c
        if r < 0:
            ref, at = outer, eo * 16 + (r + 2) * 8
        elif r < 2:
            ref, at = inner, 64 + eo * 16 + r * 8
        elif r < 6:
            ref, at = inner, eo * 32 + (r - 2) * 8
        elif r < 8:
            ref, at = inner, 96 + eo * 16 + (r - 6) * 8
        else:
            ref, at = outer, 32 + eo * 16 + (r - 8) * 8
        return ref[pl.ds(pl.multiple_of((at + tail) * LAT, 8), LAT), :]

    def potential(p):
        totals = []
        for eo in range(2):
            parts = [jnp.concatenate([level(eo, c, p, r) for r in range(-2, LEV + 2)], axis=0) for c in range(2)]
            high, low = split(jnp.concatenate(parts, axis=1))
            main = jnp.dot(jnp.concatenate([high, low, high], axis=1), main_ref[eo], preferred_element_type=F32)
            tail = jnp.dot(jnp.concatenate([high, low], axis=1), tail_ref[eo], preferred_element_type=F32)
            totals.append(jnp.concatenate([main, tail[:, :128] + tail[:, 128:]], axis=1))
        for side in range(2):
            total = totals[0] + totals[1] if side == 0 else totals[0] - totals[1]
            columns = pl.ds(side * HALF, HALF)
            for r in range(LEV):
                level_of = [total[(r + d) * LAT:(r + d + 1) * LAT] for d in range(5)]
                result[p, 0, r, :, columns] = level_of[2].astype(BF16)
                slope = (level_of[0] - level_of[4]) * (1.0 / 12.0) + (level_of[3] - level_of[1]) * (8.0 / 12.0)
                result[p, 1, r, :, columns] = slope.astype(BF16)
        pltpu.make_async_copy(result.at[p], out_ref.at[p], sem.at[p]).start()

    if LOOP:
        @pl.loop(0, POT)
        def _(p):
            potential(p)
    else:
        for p in range(POT):
            potential(p)
    for p in range(POT):
        pltpu.make_async_copy(result.at[p], out_ref.at[p], sem.at[p]).wait()


def body(coefficients, order_of_slot):
    vmem = pl.BlockSpec(memory_space=pltpu.VMEM)
    anywhere = pl.BlockSpec(memory_space=pl.ANY)
    peers = len(OFFSETS)
    got, edge, main, tail = pl.pallas_call(
        exchange_kernel,
        out_shape=[
            jax.ShapeDtypeStruct((ORD, UNITS, 8, 128), jnp.int16),
            jax.ShapeDtypeStruct((2, ORD, EDGE, 8, 128), jnp.int16),
            jax.ShapeDtypeStruct((2, 3 * LDEG, 256), BF16),
            jax.ShapeDtypeStruct((2, 2 * LDEG, 256), BF16),
        ],
        in_specs=[pl.BlockSpec(memory_space=pltpu.SMEM), vmem, anywhere],
        out_specs=[anywhere, anywhere, vmem, vmem],
        scratch_shapes=[
            pltpu.VMEM((SLOTS, LEV, POT, 2, LDEG), BF16),
            pltpu.VMEM((ORD, UNITS, 8, 128), jnp.int16),
            pltpu.VMEM((3, PAIRS * STEP, 128), F32),
            pltpu.VMEM((3, PAIRS * STEP, 128), F32),
            pltpu.VMEM((3, PAIRS, STEP + LDEG, 128), BF16),
            pltpu.VMEM((3, PAIRS, STEP + LDEG, 128), BF16),
            pltpu.VMEM((3, SLOTS * 64, 128), F32),
            pltpu.SemaphoreType.DMA((POT * LEV,)),
            pltpu.SemaphoreType.DMA,
            pltpu.SemaphoreType.DMA((peers,)),
            pltpu.SemaphoreType.DMA((peers,)),
            pltpu.SemaphoreType.DMA((ORD,)),
            pltpu.SemaphoreType.DMA((ORD,)),
            pltpu.SemaphoreType.DMA((ORD,)),
            pltpu.SemaphoreType.DMA((ORD,)),
        ],
        compiler_params=pltpu.CompilerParams(collective_id=0, has_side_effects=True),
    )(order_of_slot, order_of_slot.reshape(1, LDEG), coefficients)
    return pl.pallas_call(
        fourier_kernel,
        out_shape=jax.ShapeDtypeStruct((POT, 2, LEV, LAT, NLON), BF16),
        in_specs=[vmem] * 4,
        out_specs=anywhere,
        scratch_shapes=[
            pltpu.VMEM((64 * LAT, 128), F32),
            pltpu.VMEM((4, 32 * LAT, 128), F32),
            pltpu.VMEM((3, 128, 128), F32),
            pltpu.VMEM((3, NLAT, 128), F32),
            pltpu.VMEM((128 * LAT, 128), F32),
            pltpu.VMEM((64 * LAT, 128), F32),
            pltpu.VMEM((POT, 2, LEV, LAT, NLON), BF16),
            pltpu.SemaphoreType.DMA((POT,)),
        ],
    )(got, edge, main, tail)


def solution(mesh):
    return jax.shard_map(
        body,
        mesh=mesh,
        in_specs=(P(None, "rad", "ord", None, None), P()),
        out_specs=P(None, None, "rad", "ord", None),
        check_vma=False,
    )
```

```python
import math

import jax
import jax.numpy as jnp
from jax import lax
from jax.experimental import pallas as pl
from jax.experimental.pallas import tpu as pltpu
from jax.sharding import PartitionSpec as P

LDEG = 256
NLAT = 384
NLON = 768
HALF = NLON // 2
POT = 4
LEV = 8
SLOTS = 16
PAIRS = 8
ORD = 16
SIDE = 4
LAT = NLAT // ORD
NORTH = NLAT // 2
UNITS = 25
SCALE = 6
EDGE = 7
FIRST = (0, 3, 7, 10, 13, 16, 19, 22)
STEP = 32
GROUP = 12
LN2 = math.log(2.0)
F32 = jnp.float32
BF16 = jnp.bfloat16
MESH = pl.DeviceIdType.MESH


def split(x):
    high = x.astype(BF16)
    return high, (x - high.astype(F32)).astype(BF16)


def legendre(order_ref, own_ref, ready_copies, out_ref, fresh, spare, high_table, low_table, sums):
    first = lax.axis_index("ord") * SLOTS
    slots, orders = [0] * SLOTS, [0] * SLOTS
    for g in range(PAIRS):
        head = order_ref[first + 2 * g]
        odd = head & 1
        even_order = jnp.where(odd == 0, head, LDEG - 1 - head)
        slots[g], slots[PAIRS + g] = 2 * g + odd, 2 * g + 1 - odd
        orders[g], orders[PAIRS + g] = even_order, LDEG - 1 - even_order
    row = lax.broadcasted_iota(jnp.int32, (SLOTS, 128), 0)
    order = jnp.zeros((SLOTS, 128), jnp.int32)
    for i in range(SLOTS):
        order = jnp.where(row == i, orders[i], order)
    m = jnp.concatenate([order, order], axis=1).astype(F32)
    degree = lax.broadcasted_iota(jnp.int32, (SLOTS, LDEG), 1).astype(F32)
    msq = m * m
    raising = jnp.sqrt(jnp.maximum(4.0 * degree * degree - 1.0, 1.0) / jnp.maximum(degree * degree - msq, 1.0))
    below = degree - 1.0
    lowering = jnp.sqrt(jnp.maximum(below * below - msq, 0.0) / jnp.maximum(4.0 * below * below - 1.0, 1.0))
    lowering = raising * lowering
    factor = jnp.maximum(degree, 1.0)
    logs = jnp.log((2.0 * factor - 1.0) / (2.0 * factor))
    logs = jnp.where((degree >= 1.0) & (degree <= m), logs, 0.0)
    product = jnp.sum(logs, axis=1, keepdims=True)
    base = 0.5 * jnp.log((2.0 * m[:, :128] + 1.0) / (4.0 * math.pi)) + 0.5 * product

    lane = lax.broadcasted_iota(jnp.int32, (8, 128), 1)
    half = lane < 64

    def tiles(x):
        return [x[:8, :128], x[8:, :128], jnp.where(half, x[:8, :128], x[8:, :128])]

    theta = [math.pi * (lane.astype(F32) + 0.5) / NLAT, math.pi * ((lane & 63).astype(F32) + 128.5) / NLAT]
    cosine = [jnp.cos(t) for t in theta]
    log_sine = [jnp.log(jnp.sin(t)) for t in theta]
    cosine = [cosine[0], cosine[0], cosine[1]]
    log_sine = [log_sine[0], log_sine[0], log_sine[1]]
    order_tiles = tiles(order)
    start_scale = [b + k * s for b, k, s in zip(tiles(base), tiles(m), log_sine)]

    spare[...] = jnp.zeros_like(spare)

    def refine(stage, t, s, at):
        values = stage[t, pl.ds(s, STEP, stride=8), :]
        high, low = split(values)
        high_table[t, s, pl.ds(at, STEP), :] = high
        low_table[t, s, pl.ds(at, STEP), :] = low

    def block(step, carry):
        last, prior, scale = [list(c) for c in carry]
        for side, (stage, ready) in enumerate(((fresh, spare), (spare, fresh))):
            start = (2 * step + side) * STEP
            at = pl.multiple_of(start, STEP)
            up = pltpu.roll(raising, LDEG - start, 1)
            down = pltpu.roll(lowering, LDEG - start, 1)
            jobs = [(t, s) for t in range(3) for s in range(PAIRS)]
            for j in range(STEP):
                if j % 8 == 0:
                    growth = [jnp.exp(s) for s in scale]
                ups = tiles(jnp.broadcast_to(up[:, j:j + 1], (SLOTS, 128)))
                downs = tiles(jnp.broadcast_to(down[:, j:j + 1], (SLOTS, 128)))
                for t in range(3):
                    seed = jnp.where(order_tiles[t] == start + j, 1.0, 0.0)
                    new = (ups[t] * cosine[t]) * last[t] + (seed - downs[t] * prior[t])
                    stage[t, 8 * j:8 * j + 8, :] = new * growth[t]
                    last[t], prior[t] = new, last[t]
                if j % 8 == 7:
                    for t in range(3):
                        large = jnp.abs(last[t]) > 1e10
                        shrink = jnp.where(large, 1e-10, 1.0)
                        last[t], prior[t] = last[t] * shrink, prior[t] * shrink
                        scale[t] = scale[t] + jnp.where(large, 10.0 * math.log(10.0), 0.0)
                while jobs and len(jobs) * STEP > 24 * (STEP - 1 - j):
                    t, s = jobs.pop()
                    refine(ready, t, s, at)
        return tuple(last), tuple(prior), tuple(scale)

    blank = tuple(jnp.zeros((8, 128), F32) for _ in range(3))
    lax.fori_loop(0, LDEG // (2 * STEP), block, (blank, blank, tuple(start_scale)))
    for t in range(3):
        for s in range(PAIRS):
            refine(spare, t, s, LDEG)

    parity = lax.broadcasted_iota(jnp.int32, (64, LDEG), 1) & 1
    parity = parity.astype(F32).astype(BF16)
    wide = lax.broadcasted_iota(jnp.int32, (64, 128), 1) < 64
    for copy in ready_copies:
        copy.wait()
    top = [jnp.zeros((8, 128), F32) for _ in range(3)]
    body_rows = slice(STEP, STEP + LDEG)
    for g in range(PAIRS):
        for eo in range(2):
            left = own_ref[slots[eo * PAIRS + g]].reshape(64, LDEG)
            odd_left = left * parity
            left = jnp.concatenate([left - odd_left, odd_left], axis=0)
            right = jnp.concatenate(
                [jnp.concatenate([table[eo, g, body_rows], table[2, g, body_rows]], axis=1) for table in (high_table, low_table)],
                axis=0,
            )
            got = jnp.dot(jnp.concatenate([left, left], axis=1), right, preferred_element_type=F32)
            north = got[:64] + got[64:]
            south = got[:64] - got[64:] if eo == 0 else got[64:] - got[:64]
            near, far = north[:, 128:], south[:, 128:]
            if eo == 0:
                mixed = jnp.where(wide, near, pltpu.roll(far, 64, 1))
            else:
                mixed = jnp.where(wide, pltpu.roll(near, 64, 1), far)
            at = (2 * g + eo) * 64
            for t, part in enumerate((north[:, :128], south[:, :128], mixed)):
                sums[t, at:at + 64, :] = part
                top[t] = jnp.maximum(top[t], jnp.max(jnp.abs(part.reshape(8, 8, 128)), axis=0))

    powers = []
    for t in range(3):
        peak = jnp.max(top[t], axis=0, keepdims=True)
        power = jnp.ceil(jnp.log(jnp.maximum(peak, 1e-30)) * (1.0 / LN2) + 0.001) - 15.0
        inverse = jnp.broadcast_to(jnp.exp(-LN2 * power) * 0.9999, (128, 128))
        powers.append(power)
        for k in range(8):
            if k < 2:
                picks = [(2 * q + k, eo, r) for q in range(4) for eo in range(2) for r in (0, 1)]
            elif k < 4:
                picks = [(2 * q + k - 2, eo, r) for q in range(4) for eo in range(2) for r in (6, 7)]
            else:
                picks = [(4 * h + k - 4, eo, r) for h in range(2) for eo in range(2) for r in (2, 3, 4, 5)]
            pieces = [sums[t, (2 * g + eo) * 64 + 8 * r:(2 * g + eo) * 64 + 8 * r + 8, :] for g, eo, r in picks]
            coded = jnp.round(jnp.concatenate(pieces, axis=0) * inverse)
            coded = coded.T.astype(jnp.int32)
            if t < 2:
                spans = [(d, 0, 3, LAT * d) for d in range(5)] + [(5, 0, 1, 120)]
                spans = [(d if t == 0 else ORD - 1 - d, lo, hi, at) for d, lo, hi, at in spans]
            else:
                spans = [(5, 1, 3, 0), (6, 0, 3, 16), (7, 0, 3, 40)]
                spans = spans + [(ORD - 1 - d, lo, hi, at + 64) for d, lo, hi, at in spans]
            for d, lo, hi, at in spans:
                part = coded[at:at + 8 * (hi - lo)].reshape(hi - lo, 8, 128)
                out_ref[d, FIRST[k] + lo:FIRST[k] + hi] = part.astype(jnp.int16)
    sublane = lax.broadcasted_iota(jnp.int32, (8, 128), 0)
    power = jnp.where(sublane == 0, powers[0], jnp.where(sublane == 1, powers[1], powers[2]))
    power = power.astype(jnp.int32).astype(jnp.int16)
    for d in range(ORD):
        out_ref[d, SCALE] = power


def turn(product):
    rest = product - NLON * jnp.floor(product * (1.0 / NLON))
    quarter = jnp.floor(rest * (1.0 / 192.0) + 0.5)
    x = (rest - 192.0 * quarter) * (2.0 * math.pi / NLON)
    y = x * x
    sine = x * (1.0 + y * (-1.0 / 6.0 + y * (1.0 / 120.0 + y * (-1.0 / 5040.0 + y * (1.0 / 362880.0)))))
    cosine = 1.0 + y * (-0.5 + y * (1.0 / 24.0 + y * (-1.0 / 720.0 + y * (1.0 / 40320.0 - y * (1.0 / 3628800.0)))))
    swap = (quarter == 1.0) | (quarter == 3.0)
    first = jnp.where(swap, sine, cosine)
    second = jnp.where(swap, cosine, sine)
    first = jnp.where((quarter == 1.0) | (quarter == 2.0), -first, first)
    second = jnp.where((quarter == 2.0) | (quarter == 3.0), -second, second)
    return first, second


def wave_tables(order_ref, main_ref, tail_ref):
    row = lax.broadcasted_iota(jnp.int32, (128, LDEG), 0)
    lane = lax.broadcasted_iota(jnp.int32, (128, LDEG), 1)
    source = (row & 15) * SLOTS + 2 * (row >> 4)
    heads = jnp.broadcast_to(order_ref[...], (128, LDEG)).astype(F32)
    head = jnp.sum(jnp.where(lane == source, heads, 0.0), axis=1, keepdims=True)
    even = jnp.where(head - 2.0 * jnp.floor(0.5 * head) == 0.0, head, LDEG - 1 - head)
    for eo in range(2):
        order = jnp.broadcast_to(even if eo == 0 else LDEG - 1 - even, (128, 128))
        weight = jnp.where(order == 0.0, 1.0, 2.0)
        for j in range(3):
            k = lax.broadcasted_iota(jnp.int32, (128, 128), 1).astype(F32) + 128.0 * j
            cosine, sine = turn(order * k)
            for c, wave in enumerate((weight * cosine, -weight * sine)):
                high, low = split(wave)
                at = c * 128
                if j < 2:
                    columns = pl.ds(128 * j, 128)
                    main_ref[eo, at:at + 128, columns] = high
                    main_ref[eo, LDEG + at:LDEG + at + 128, columns] = high
                    main_ref[eo, 2 * LDEG + at:2 * LDEG + at + 128, columns] = low
                else:
                    for b in range(2):
                        tail_ref[eo, b * LDEG + at:b * LDEG + at + 128, :128] = high
                        tail_ref[eo, b * LDEG + at:b * LDEG + at + 128, 128:] = low


OFFSETS = [(dy, dx) for dy in range(SIDE) for dx in range(SIDE) if (dy, dx) != (0, 0)]
OFFSETS.sort(key=lambda o: -min(o[0], SIDE - o[0]) - min(o[1], SIDE - o[1]))


def value(coded):
    return coded.astype(jnp.int32).astype(F32)


def take(coded):
    return value(coded).reshape(LAT, 128)


def place_of_latitudes():
    place = lax.axis_index("ord")
    mirror = place >= ORD // 2
    first = jnp.where(mirror, ORD - 1 - place, place) * LAT

    def place(i):
        at = jnp.where(mirror, LAT - 1 - i, i)
        north = first + at
        row = jnp.where(north < 128, north + jnp.where(mirror, 128, 0), north + 128 + jnp.where(mirror, 64, 0))
        return at, row

    return place


def turn_scales(scales, turned):
    for t in range(3):
        row = scales[pl.ds(t, ORD, stride=8), :]
        turned[128 * t:128 * t + 128, :] = jnp.concatenate([row] * 8, axis=0).T


def turner(parts):
    width = 128 // parts
    lane = lax.broadcasted_iota(jnp.int32, (width, 256), 1)
    row = lax.broadcasted_iota(jnp.int32, (width, 256), 0)
    pick = jnp.where((lane & (width - 1)) == row, 1.0, 0.0).astype(BF16)

    def turn_blocks(blocks):
        rows = []
        for block in blocks:
            high, low = split(block)
            group = lax.broadcasted_iota(jnp.int32, block.shape, 1) // width
            for q in range(parts):
                keep = jnp.where(group == q, 1.0, 0.0).astype(BF16)
                rows.append(jnp.concatenate([high * keep, low * keep], axis=1))
        rows = jnp.concatenate(rows, axis=0)
        return lax.dot_general(pick, rows, (((1,), (1,)), ((), ())), preferred_element_type=F32)

    return turn_blocks


def exchange_kernel(
    order_ref, heads_ref, coefficients_ref, inner_ref, edge_ref, main_ref, tail_ref,
    own_ref, coded_ref, fresh, spare, high_table, low_table, sums, got_ref, middle, edges, scales, turned, inner,
    load_sem, out_sem, send_sem, recv_sem, up_send, up_recv, down_send, down_recv,
):
    me = lax.axis_index("ord")
    y, x = me // SIDE, me % SIDE
    rad = lax.axis_index("rad")
    count = lax.axis_size("rad")
    upper, lower = (rad + 1) % count, (rad + count - 1) % count

    def other(dy, dx):
        return (y + dy) % SIDE * SIDE + (x + dx) % SIDE

    barrier = pltpu.get_barrier_semaphore()
    for dy, dx in OFFSETS:
        pl.semaphore_signal(barrier, inc=1, device_id={"ord": other(dy, dx)}, device_id_type=MESH)
    for neighbour in (lower, upper):
        pl.semaphore_signal(barrier, inc=1, device_id={"rad": neighbour}, device_id_type=MESH)

    loads = []
    for p in range(POT):
        for r in range(LEV):
            copy = pltpu.make_async_copy(coefficients_ref.at[p, r], own_ref.at[:, r, p], load_sem.at[p * LEV + r])
            copy.start()
            loads.append(copy)
    legendre(order_ref, own_ref, loads, coded_ref, fresh, spare, high_table, low_table, sums)
    pl.semaphore_wait(barrier, len(OFFSETS) + 2)

    sends = []
    for n, (dy, dx) in enumerate(OFFSETS):
        peer = other(dy, dx)
        copy = pltpu.make_async_remote_copy(
            src_ref=coded_ref.at[peer], dst_ref=got_ref.at[me], send_sem=send_sem.at[n], recv_sem=recv_sem.at[n],
            device_id={"ord": peer}, device_id_type=MESH,
        )
        copy.start()
        sends.append(copy)
    passed = []

    def pass_on(block, source, n):
        down = pltpu.make_async_remote_copy(
            src_ref=block.at[0:EDGE], dst_ref=edge_ref.at[1, source], send_sem=down_send.at[n], recv_sem=down_recv.at[n],
            device_id={"rad": lower}, device_id_type=MESH,
        )
        up = pltpu.make_async_remote_copy(
            src_ref=block.at[SCALE:SCALE + EDGE], dst_ref=edge_ref.at[0, source], send_sem=up_send.at[n], recv_sem=up_recv.at[n],
            device_id={"rad": upper}, device_id_type=MESH,
        )
        down.start()
        up.start()
        passed.extend([down, up])

    def unpack(ref, source):
        for k in range(4):
            at = pl.multiple_of((k * ORD + source) * LAT, 8)
            middle[pl.ds(at, LAT), :] = take(ref[source, 13 + 3 * k:16 + 3 * k])
        for k in range(2):
            at = pl.multiple_of((k * ORD + source) * LAT, 8)
            edges[0, pl.ds(at, LAT), :] = take(ref[source, 3 * k:3 * k + 3])
            edges[1, pl.ds(at, LAT), :] = take(ref[source, 7 + 3 * k:10 + 3 * k])
        scales[pl.ds(pl.multiple_of(8 * source, 8), 8), :] = value(ref[source, SCALE])

    pass_on(coded_ref.at[me], me, len(OFFSETS))
    wave_tables(heads_ref, main_ref, tail_ref)
    unpack(coded_ref, me)
    for n, (dy, dx) in enumerate(OFFSETS):
        sends[n].wait_recv()
        source = other(SIDE - dy, SIDE - dx)
        pass_on(got_ref.at[source], source, n)
        unpack(got_ref, source)
    turn_scales(scales, turned)
    place = place_of_latitudes()
    turn_middle, turn_edges = turner(2), turner(4)

    @pl.loop(0, LAT // GROUP)
    def _(n):
        for j in range(GROUP):
            i = n * GROUP + j
            at, row = place(i)
            unit = jnp.exp(LN2 * turned[pl.ds(row, 1), :]) * (1.0 / 0.9999)
            mid = turn_middle([middle[pl.ds(at, 64, stride=LAT), :]])
            ends = turn_edges([edges[e, pl.ds(at, 32, stride=LAT), :] for e in range(2)])
            inner[pl.ds(i, 64, stride=LAT), :] = mid * unit
            inner[pl.ds(64 * LAT + i, 32, stride=LAT), :] = ends[:, :128] * unit
            inner[pl.ds(96 * LAT + i, 32, stride=LAT), :] = ends[:, 128:] * unit

    result = pltpu.make_async_copy(inner, inner_ref, out_sem)
    result.start()
    for copy in sends:
        copy.wait_send()
    for copy in passed:
        copy.wait()
    result.wait()


def fourier_kernel(inner_hbm, edge_hbm, main_hbm, tail_hbm, out_ref, inner, edge_ref, main_ref, tail_ref, edges, scales, turned, outer, result, load_sem, sem):
    loads = [
        pltpu.make_async_copy(source, target, load_sem.at[n])
        for n, (source, target) in enumerate(((edge_hbm, edge_ref), (inner_hbm, inner), (main_hbm, main_ref), (tail_hbm, tail_ref)))
    ]
    for copy in loads:
        copy.start()
    loads[0].wait()
    rad = lax.axis_index("rad")
    count = lax.axis_size("rad")
    keep_low = jnp.where(rad == 0, 0.0, 1.0) * (1.0 / 0.9999)
    keep_high = jnp.where(rad == count - 1, 0.0, 1.0) * (1.0 / 0.9999)
    for s in range(ORD):
        for k in range(2):
            at = (k * ORD + s) * LAT
            edges[0, at:at + LAT, :] = take(edge_ref[0, s, 1 + 3 * k:4 + 3 * k])
            edges[1, at:at + LAT, :] = take(edge_ref[1, s, 3 * k:3 * k + 3])
        scales[0, 8 * s:8 * s + 8, :] = value(edge_ref[0, s, 0])
        scales[1, 8 * s:8 * s + 8, :] = value(edge_ref[1, s, SCALE])
    for e in range(2):
        turn_scales(scales.at[e], turned.at[e])
    place = place_of_latitudes()
    turn_edges = turner(4)

    @pl.loop(0, LAT // GROUP)
    def _(n):
        for j in range(GROUP):
            i = n * GROUP + j
            at, row = place(i)
            below = jnp.exp(LN2 * turned[0, pl.ds(row, 1), :]) * keep_low
            above = jnp.exp(LN2 * turned[1, pl.ds(row, 1), :]) * keep_high
            ends = turn_edges([edges[e, pl.ds(at, 32, stride=LAT), :] for e in range(2)])
            outer[pl.ds(i, 32, stride=LAT), :] = ends[:, :128] * below
            outer[pl.ds(32 * LAT + i, 32, stride=LAT), :] = ends[:, 128:] * above

    for copy in loads[1:]:
        copy.wait()

    def level(eo, c, p, r):
        tail = 2 * p + c
        if r < 0:
            ref, at = outer, eo * 16 + (r + 2) * 8
        elif r < 2:
            ref, at = inner, 64 + eo * 16 + r * 8
        elif r < 6:
            ref, at = inner, eo * 32 + (r - 2) * 8
        elif r < 8:
            ref, at = inner, 96 + eo * 16 + (r - 6) * 8
        else:
            ref, at = outer, 32 + eo * 16 + (r - 8) * 8
        return ref[pl.ds(pl.multiple_of((at + tail) * LAT, 8), LAT), :]

    def out_copy(p, side):
        columns = pl.ds(side * HALF, HALF)
        return pltpu.make_async_copy(result.at[p, :, :, :, columns], out_ref.at[p, :, :, :, columns], sem.at[p, side])

    def potential(p):
        totals = []
        for eo in range(2):
            parts = [jnp.concatenate([level(eo, c, p, r) for r in range(-2, LEV + 2)], axis=0) for c in range(2)]
            high, low = split(jnp.concatenate(parts, axis=1))
            main = jnp.dot(jnp.concatenate([high, low, high], axis=1), main_ref[eo], preferred_element_type=F32)
            tail = jnp.dot(jnp.concatenate([high, low], axis=1), tail_ref[eo], preferred_element_type=F32)
            totals.append(jnp.concatenate([main, tail[:, :128] + tail[:, 128:]], axis=1))
        for side in range(2):
            total = totals[0] + totals[1] if side == 0 else totals[0] - totals[1]
            columns = pl.ds(side * HALF, HALF)
            for r in range(LEV):
                level_of = [total[(r + d) * LAT:(r + d + 1) * LAT] for d in range(5)]
                result[p, 0, r, :, columns] = level_of[2].astype(BF16)
                slope = (level_of[0] - level_of[4]) * (1.0 / 12.0) + (level_of[3] - level_of[1]) * (8.0 / 12.0)
                result[p, 1, r, :, columns] = slope.astype(BF16)
            out_copy(p, side).start()

    @pl.loop(0, POT)
    def _(p):
        potential(p)

    for p in range(POT):
        for side in range(2):
            out_copy(p, side).wait()


def body(coefficients, order_of_slot):
    vmem = pl.BlockSpec(memory_space=pltpu.VMEM)
    anywhere = pl.BlockSpec(memory_space=pl.ANY)
    peers = len(OFFSETS)
    inner, edge, main, tail = pl.pallas_call(
        exchange_kernel,
        out_shape=[
            jax.ShapeDtypeStruct((128 * LAT, 128), F32),
            jax.ShapeDtypeStruct((2, ORD, EDGE, 8, 128), jnp.int16),
            jax.ShapeDtypeStruct((2, 3 * LDEG, 256), BF16),
            jax.ShapeDtypeStruct((2, 2 * LDEG, 256), BF16),
        ],
        in_specs=[pl.BlockSpec(memory_space=pltpu.SMEM), vmem, anywhere],
        out_specs=[anywhere, anywhere, vmem, vmem],
        scratch_shapes=[
            pltpu.VMEM((SLOTS, LEV, POT, 2, LDEG), BF16),
            pltpu.VMEM((ORD, UNITS, 8, 128), jnp.int16),
            pltpu.VMEM((3, PAIRS * STEP, 128), F32),
            pltpu.VMEM((3, PAIRS * STEP, 128), F32),
            pltpu.VMEM((3, PAIRS, STEP + LDEG, 128), BF16),
            pltpu.VMEM((3, PAIRS, STEP + LDEG, 128), BF16),
            pltpu.VMEM((3, SLOTS * 64, 128), F32),
            pltpu.VMEM((ORD, UNITS, 8, 128), jnp.int16),
            pltpu.VMEM((64 * LAT, 128), F32),
            pltpu.VMEM((2, 32 * LAT, 128), F32),
            pltpu.VMEM((128, 128), F32),
            pltpu.VMEM((NLAT, 128), F32),
            pltpu.VMEM((128 * LAT, 128), F32),
            pltpu.SemaphoreType.DMA((POT * LEV,)),
            pltpu.SemaphoreType.DMA,
            pltpu.SemaphoreType.DMA((peers,)),
            pltpu.SemaphoreType.DMA((peers,)),
            pltpu.SemaphoreType.DMA((ORD,)),
            pltpu.SemaphoreType.DMA((ORD,)),
            pltpu.SemaphoreType.DMA((ORD,)),
            pltpu.SemaphoreType.DMA((ORD,)),
        ],
        compiler_params=pltpu.CompilerParams(collective_id=0, has_side_effects=True),
    )(order_of_slot, order_of_slot.reshape(1, LDEG), coefficients)
    return pl.pallas_call(
        fourier_kernel,
        out_shape=jax.ShapeDtypeStruct((POT, 2, LEV, LAT, NLON), BF16),
        in_specs=[anywhere] * 4,
        out_specs=anywhere,
        scratch_shapes=[
            pltpu.VMEM((128 * LAT, 128), F32),
            pltpu.VMEM((2, ORD, EDGE, 8, 128), jnp.int16),
            pltpu.VMEM((2, 3 * LDEG, 256), BF16),
            pltpu.VMEM((2, 2 * LDEG, 256), BF16),
            pltpu.VMEM((2, 32 * LAT, 128), F32),
            pltpu.VMEM((2, 128, 128), F32),
            pltpu.VMEM((2, NLAT, 128), F32),
            pltpu.VMEM((64 * LAT, 128), F32),
            pltpu.VMEM((POT, 2, LEV, LAT, NLON), BF16),
            pltpu.SemaphoreType.DMA((4,)),
            pltpu.SemaphoreType.DMA((POT, 2)),
        ],
    )(inner, edge, main, tail)


def solution(mesh):
    return jax.shard_map(
        body,
        mesh=mesh,
        in_specs=(P(None, "rad", "ord", None, None), P()),
        out_specs=P(None, None, "rad", "ord", None),
        check_vma=False,
    )
```

```python
import math

import jax
import jax.numpy as jnp
from jax import lax
from jax.experimental import pallas as pl
from jax.experimental.pallas import tpu as pltpu
from jax.sharding import PartitionSpec as P

LDEG = 256
NLAT = 384
NLON = 768
HALF = NLON // 2
POT = 4
LEV = 8
SLOTS = 16
PAIRS = 8
ORD = 16
SIDE = 4
LAT = NLAT // ORD
NORTH = NLAT // 2
UNITS = 25
SCALE = 6
EDGE = 7
FIRST = (0, 3, 7, 10, 13, 16, 19, 22)
STEP = 32
GROUP = 12
LN2 = math.log(2.0)
F32 = jnp.float32
BF16 = jnp.bfloat16
MESH = pl.DeviceIdType.MESH


def split(x):
    high = x.astype(BF16)
    return high, (x - high.astype(F32)).astype(BF16)


def legendre(order_ref, own_ref, ready_copies, out_ref, fresh, spare, high_table, low_table, sums):
    first = lax.axis_index("ord") * SLOTS
    slots, orders = [0] * SLOTS, [0] * SLOTS
    for g in range(PAIRS):
        head = order_ref[first + 2 * g]
        odd = head & 1
        even_order = jnp.where(odd == 0, head, LDEG - 1 - head)
        slots[g], slots[PAIRS + g] = 2 * g + odd, 2 * g + 1 - odd
        orders[g], orders[PAIRS + g] = even_order, LDEG - 1 - even_order
    row = lax.broadcasted_iota(jnp.int32, (SLOTS, 128), 0)
    order = jnp.zeros((SLOTS, 128), jnp.int32)
    for i in range(SLOTS):
        order = jnp.where(row == i, orders[i], order)
    m = jnp.concatenate([order, order], axis=1).astype(F32)
    degree = lax.broadcasted_iota(jnp.int32, (SLOTS, LDEG), 1).astype(F32)
    msq = m * m
    raising = jnp.sqrt(jnp.maximum(4.0 * degree * degree - 1.0, 1.0) / jnp.maximum(degree * degree - msq, 1.0))
    below = degree - 1.0
    lowering = jnp.sqrt(jnp.maximum(below * below - msq, 0.0) / jnp.maximum(4.0 * below * below - 1.0, 1.0))
    lowering = raising * lowering
    factor = jnp.maximum(degree, 1.0)
    logs = jnp.log((2.0 * factor - 1.0) / (2.0 * factor))
    logs = jnp.where((degree >= 1.0) & (degree <= m), logs, 0.0)
    product = jnp.sum(logs, axis=1, keepdims=True)
    base = 0.5 * jnp.log((2.0 * m[:, :128] + 1.0) / (4.0 * math.pi)) + 0.5 * product

    lane = lax.broadcasted_iota(jnp.int32, (8, 128), 1)
    half = lane < 64

    def tiles(x):
        return [x[:8, :128], x[8:, :128], jnp.where(half, x[:8, :128], x[8:, :128])]

    theta = [math.pi * (lane.astype(F32) + 0.5) / NLAT, math.pi * ((lane & 63).astype(F32) + 128.5) / NLAT]
    cosine = [jnp.cos(t) for t in theta]
    log_sine = [jnp.log(jnp.sin(t)) for t in theta]
    cosine = [cosine[0], cosine[0], cosine[1]]
    log_sine = [log_sine[0], log_sine[0], log_sine[1]]
    order_tiles = tiles(order)
    start_scale = [b + k * s for b, k, s in zip(tiles(base), tiles(m), log_sine)]

    spare[...] = jnp.zeros_like(spare)

    def refine(stage, t, s, at):
        values = stage[t, pl.ds(s, STEP, stride=8), :]
        high, low = split(values)
        high_table[t, s, pl.ds(at, STEP), :] = high
        low_table[t, s, pl.ds(at, STEP), :] = low

    def block(step, carry):
        last, prior, scale = [list(c) for c in carry]
        for side, (stage, ready) in enumerate(((fresh, spare), (spare, fresh))):
            start = (2 * step + side) * STEP
            at = pl.multiple_of(start, STEP)
            up = pltpu.roll(raising, LDEG - start, 1)
            down = pltpu.roll(lowering, LDEG - start, 1)
            jobs = [(t, s) for t in range(3) for s in range(PAIRS)]
            for j in range(STEP):
                if j % 8 == 0:
                    growth = [jnp.exp(s) for s in scale]
                ups = tiles(jnp.broadcast_to(up[:, j:j + 1], (SLOTS, 128)))
                downs = tiles(jnp.broadcast_to(down[:, j:j + 1], (SLOTS, 128)))
                for t in range(3):
                    seed = jnp.where(order_tiles[t] == start + j, 1.0, 0.0)
                    new = (ups[t] * cosine[t]) * last[t] + (seed - downs[t] * prior[t])
                    stage[t, 8 * j:8 * j + 8, :] = new * growth[t]
                    last[t], prior[t] = new, last[t]
                if j % 8 == 7:
                    for t in range(3):
                        large = jnp.abs(last[t]) > 1e10
                        shrink = jnp.where(large, 1e-10, 1.0)
                        last[t], prior[t] = last[t] * shrink, prior[t] * shrink
                        scale[t] = scale[t] + jnp.where(large, 10.0 * math.log(10.0), 0.0)
                while jobs and len(jobs) * STEP > 24 * (STEP - 1 - j):
                    t, s = jobs.pop()
                    refine(ready, t, s, at)
        return tuple(last), tuple(prior), tuple(scale)

    blank = tuple(jnp.zeros((8, 128), F32) for _ in range(3))
    lax.fori_loop(0, LDEG // (2 * STEP), block, (blank, blank, tuple(start_scale)))
    for t in range(3):
        for s in range(PAIRS):
            refine(spare, t, s, LDEG)

    parity = lax.broadcasted_iota(jnp.int32, (64, LDEG), 1) & 1
    parity = parity.astype(F32).astype(BF16)
    wide = lax.broadcasted_iota(jnp.int32, (64, 128), 1) < 64
    for copy in ready_copies:
        copy.wait()
    top = [jnp.zeros((8, 128), F32) for _ in range(3)]
    body_rows = slice(STEP, STEP + LDEG)
    for g in range(PAIRS):
        for eo in range(2):
            left = own_ref[slots[eo * PAIRS + g]].reshape(64, LDEG)
            odd_left = left * parity
            left = jnp.concatenate([left - odd_left, odd_left], axis=0)
            right = jnp.concatenate(
                [jnp.concatenate([table[eo, g, body_rows], table[2, g, body_rows]], axis=1) for table in (high_table, low_table)],
                axis=0,
            )
            got = jnp.dot(jnp.concatenate([left, left], axis=1), right, preferred_element_type=F32)
            north = got[:64] + got[64:]
            south = got[:64] - got[64:] if eo == 0 else got[64:] - got[:64]
            near, far = north[:, 128:], south[:, 128:]
            if eo == 0:
                mixed = jnp.where(wide, near, pltpu.roll(far, 64, 1))
            else:
                mixed = jnp.where(wide, pltpu.roll(near, 64, 1), far)
            at = (2 * g + eo) * 64
            for t, part in enumerate((north[:, :128], south[:, :128], mixed)):
                sums[t, at:at + 64, :] = part
                top[t] = jnp.maximum(top[t], jnp.max(jnp.abs(part.reshape(8, 8, 128)), axis=0))

    powers = []
    for t in range(3):
        peak = jnp.max(top[t], axis=0, keepdims=True)
        power = jnp.ceil(jnp.log(jnp.maximum(peak, 1e-30)) * (1.0 / LN2) + 0.001) - 15.0
        inverse = jnp.broadcast_to(jnp.exp(-LN2 * power) * 0.9999, (128, 128))
        powers.append(power)
        for k in range(8):
            if k < 2:
                picks = [(2 * q + k, eo, r) for q in range(4) for eo in range(2) for r in (0, 1)]
            elif k < 4:
                picks = [(2 * q + k - 2, eo, r) for q in range(4) for eo in range(2) for r in (6, 7)]
            else:
                picks = [(4 * h + k - 4, eo, r) for h in range(2) for eo in range(2) for r in (2, 3, 4, 5)]
            pieces = [sums[t, (2 * g + eo) * 64 + 8 * r:(2 * g + eo) * 64 + 8 * r + 8, :] for g, eo, r in picks]
            coded = jnp.round(jnp.concatenate(pieces, axis=0) * inverse)
            coded = coded.T.astype(jnp.int32)
            if t < 2:
                spans = [(d, 0, 3, LAT * d) for d in range(5)] + [(5, 0, 1, 120)]
                spans = [(d if t == 0 else ORD - 1 - d, lo, hi, at) for d, lo, hi, at in spans]
            else:
                spans = [(5, 1, 3, 0), (6, 0, 3, 16), (7, 0, 3, 40)]
                spans = spans + [(ORD - 1 - d, lo, hi, at + 64) for d, lo, hi, at in spans]
            for d, lo, hi, at in spans:
                part = coded[at:at + 8 * (hi - lo)].reshape(hi - lo, 8, 128)
                out_ref[d, FIRST[k] + lo:FIRST[k] + hi] = part.astype(jnp.int16)
    sublane = lax.broadcasted_iota(jnp.int32, (8, 128), 0)
    power = jnp.where(sublane == 0, powers[0], jnp.where(sublane == 1, powers[1], powers[2]))
    power = power.astype(jnp.int32).astype(jnp.int16)
    for d in range(ORD):
        out_ref[d, SCALE] = power


def turn(product):
    rest = product - NLON * jnp.floor(product * (1.0 / NLON))
    quarter = jnp.floor(rest * (1.0 / 192.0) + 0.5)
    x = (rest - 192.0 * quarter) * (2.0 * math.pi / NLON)
    y = x * x
    sine = x * (1.0 + y * (-1.0 / 6.0 + y * (1.0 / 120.0 + y * (-1.0 / 5040.0 + y * (1.0 / 362880.0)))))
    cosine = 1.0 + y * (-0.5 + y * (1.0 / 24.0 + y * (-1.0 / 720.0 + y * (1.0 / 40320.0 - y * (1.0 / 3628800.0)))))
    swap = (quarter == 1.0) | (quarter == 3.0)
    first = jnp.where(swap, sine, cosine)
    second = jnp.where(swap, cosine, sine)
    first = jnp.where((quarter == 1.0) | (quarter == 2.0), -first, first)
    second = jnp.where((quarter == 2.0) | (quarter == 3.0), -second, second)
    return first, second


def wave_tables(order_ref, main_ref, tail_ref):
    row = lax.broadcasted_iota(jnp.int32, (128, LDEG), 0)
    lane = lax.broadcasted_iota(jnp.int32, (128, LDEG), 1)
    source = (row & 15) * SLOTS + 2 * (row >> 4)
    heads = jnp.broadcast_to(order_ref[...], (128, LDEG)).astype(F32)
    head = jnp.sum(jnp.where(lane == source, heads, 0.0), axis=1, keepdims=True)
    even = jnp.where(head - 2.0 * jnp.floor(0.5 * head) == 0.0, head, LDEG - 1 - head)
    for eo in range(2):
        order = jnp.broadcast_to(even if eo == 0 else LDEG - 1 - even, (128, 128))
        weight = jnp.where(order == 0.0, 1.0, 2.0)
        for j in range(3):
            k = lax.broadcasted_iota(jnp.int32, (128, 128), 1).astype(F32) + 128.0 * j
            cosine, sine = turn(order * k)
            for c, wave in enumerate((weight * cosine, -weight * sine)):
                high, low = split(wave)
                at = c * 128
                if j < 2:
                    columns = pl.ds(128 * j, 128)
                    main_ref[eo, at:at + 128, columns] = high
                    main_ref[eo, LDEG + at:LDEG + at + 128, columns] = high
                    main_ref[eo, 2 * LDEG + at:2 * LDEG + at + 128, columns] = low
                else:
                    for b in range(2):
                        tail_ref[eo, b * LDEG + at:b * LDEG + at + 128, :128] = high
                        tail_ref[eo, b * LDEG + at:b * LDEG + at + 128, 128:] = low


OFFSETS = [(dy, dx) for dy in range(SIDE) for dx in range(SIDE) if (dy, dx) != (0, 0)]
OFFSETS.sort(key=lambda o: -min(o[0], SIDE - o[0]) - min(o[1], SIDE - o[1]))


def value(coded):
    return coded.astype(jnp.int32).astype(F32)


def take(coded):
    return value(coded).reshape(LAT, 128)


def place_of_latitudes():
    place = lax.axis_index("ord")
    mirror = place >= ORD // 2
    first = jnp.where(mirror, ORD - 1 - place, place) * LAT

    def place(i):
        at = jnp.where(mirror, LAT - 1 - i, i)
        north = first + at
        row = jnp.where(north < 128, north + jnp.where(mirror, 128, 0), north + 128 + jnp.where(mirror, 64, 0))
        return at, row

    return place


def turn_scales(scales, turned):
    for t in range(3):
        row = scales[pl.ds(t, ORD, stride=8), :]
        turned[128 * t:128 * t + 128, :] = jnp.concatenate([row] * 8, axis=0).T


def turner(parts):
    width = 128 // parts
    lane = lax.broadcasted_iota(jnp.int32, (width, 256), 1)
    row = lax.broadcasted_iota(jnp.int32, (width, 256), 0)
    pick = jnp.where((lane & (width - 1)) == row, 1.0, 0.0).astype(BF16)

    def turn_blocks(blocks):
        rows = []
        for block in blocks:
            high, low = split(block)
            group = lax.broadcasted_iota(jnp.int32, block.shape, 1) // width
            for q in range(parts):
                keep = jnp.where(group == q, 1.0, 0.0).astype(BF16)
                rows.append(jnp.concatenate([high * keep, low * keep], axis=1))
        rows = jnp.concatenate(rows, axis=0)
        return lax.dot_general(pick, rows, (((1,), (1,)), ((), ())), preferred_element_type=F32)

    return turn_blocks


def exchange_kernel(
    order_ref, heads_ref, coefficients_ref, inner_ref, edge_ref, main_out, tail_out,
    main_ref, tail_ref, own_ref, coded_ref, fresh, spare, high_table, low_table, sums, got_ref, middle, edges, scales, turned, inner,
    load_sem, out_sem, wave_sem, send_sem, recv_sem, up_send, up_recv, down_send, down_recv,
):
    me = lax.axis_index("ord")
    y, x = me // SIDE, me % SIDE
    rad = lax.axis_index("rad")
    count = lax.axis_size("rad")
    upper, lower = (rad + 1) % count, (rad + count - 1) % count

    def other(dy, dx):
        return (y + dy) % SIDE * SIDE + (x + dx) % SIDE

    barrier = pltpu.get_barrier_semaphore()
    for dy, dx in OFFSETS:
        pl.semaphore_signal(barrier, inc=1, device_id={"ord": other(dy, dx)}, device_id_type=MESH)
    for neighbour in (lower, upper):
        pl.semaphore_signal(barrier, inc=1, device_id={"rad": neighbour}, device_id_type=MESH)

    loads = []
    for p in range(POT):
        for r in range(LEV):
            copy = pltpu.make_async_copy(coefficients_ref.at[p, r], own_ref.at[:, r, p], load_sem.at[p * LEV + r])
            copy.start()
            loads.append(copy)
    legendre(order_ref, own_ref, loads, coded_ref, fresh, spare, high_table, low_table, sums)
    pl.semaphore_wait(barrier, len(OFFSETS) + 2)

    sends = []
    for n, (dy, dx) in enumerate(OFFSETS):
        peer = other(dy, dx)
        copy = pltpu.make_async_remote_copy(
            src_ref=coded_ref.at[peer], dst_ref=got_ref.at[me], send_sem=send_sem.at[n], recv_sem=recv_sem.at[n],
            device_id={"ord": peer}, device_id_type=MESH,
        )
        copy.start()
        sends.append(copy)
    passed = []

    def pass_on(block, source, n):
        down = pltpu.make_async_remote_copy(
            src_ref=block.at[0:EDGE], dst_ref=edge_ref.at[1, source], send_sem=down_send.at[n], recv_sem=down_recv.at[n],
            device_id={"rad": lower}, device_id_type=MESH,
        )
        up = pltpu.make_async_remote_copy(
            src_ref=block.at[SCALE:SCALE + EDGE], dst_ref=edge_ref.at[0, source], send_sem=up_send.at[n], recv_sem=up_recv.at[n],
            device_id={"rad": upper}, device_id_type=MESH,
        )
        down.start()
        up.start()
        passed.extend([down, up])

    def unpack(ref, source):
        for k in range(4):
            at = pl.multiple_of((k * ORD + source) * LAT, 8)
            middle[pl.ds(at, LAT), :] = take(ref[source, 13 + 3 * k:16 + 3 * k])
        for k in range(2):
            at = pl.multiple_of((k * ORD + source) * LAT, 8)
            edges[0, pl.ds(at, LAT), :] = take(ref[source, 3 * k:3 * k + 3])
            edges[1, pl.ds(at, LAT), :] = take(ref[source, 7 + 3 * k:10 + 3 * k])
        scales[pl.ds(pl.multiple_of(8 * source, 8), 8), :] = value(ref[source, SCALE])

    pass_on(coded_ref.at[me], me, len(OFFSETS))
    wave_tables(heads_ref, main_ref, tail_ref)
    waves = [
        pltpu.make_async_copy(main_ref, main_out, wave_sem.at[0]),
        pltpu.make_async_copy(tail_ref, tail_out, wave_sem.at[1]),
    ]
    for copy in waves:
        copy.start()
    unpack(coded_ref, me)
    for n, (dy, dx) in reversed(list(enumerate(OFFSETS))):
        sends[n].wait_recv()
        source = other(SIDE - dy, SIDE - dx)
        pass_on(got_ref.at[source], source, n)
        unpack(got_ref, source)
    turn_scales(scales, turned)
    place = place_of_latitudes()
    turn_middle, turn_edges = turner(2), turner(4)

    @pl.loop(0, LAT // GROUP)
    def _(n):
        for j in range(GROUP):
            i = n * GROUP + j
            at, row = place(i)
            unit = jnp.exp(LN2 * turned[pl.ds(row, 1), :]) * (1.0 / 0.9999)
            mid = turn_middle([middle[pl.ds(at, 64, stride=LAT), :]])
            ends = turn_edges([edges[e, pl.ds(at, 32, stride=LAT), :] for e in range(2)])
            inner[pl.ds(i, 64, stride=LAT), :] = mid * unit
            inner[pl.ds(64 * LAT + i, 32, stride=LAT), :] = ends[:, :128] * unit
            inner[pl.ds(96 * LAT + i, 32, stride=LAT), :] = ends[:, 128:] * unit

    result = pltpu.make_async_copy(inner, inner_ref, out_sem)
    result.start()
    for copy in sends:
        copy.wait_send()
    for copy in passed:
        copy.wait()
    for copy in waves:
        copy.wait()
    result.wait()


def fourier_kernel(inner_hbm, edge_hbm, main_hbm, tail_hbm, out_ref, inner, edge_ref, main_ref, tail_ref, edges, scales, turned, outer, result, load_sem, sem):
    loads = [
        pltpu.make_async_copy(source, target, load_sem.at[n])
        for n, (source, target) in enumerate(((edge_hbm, edge_ref), (inner_hbm, inner), (main_hbm, main_ref), (tail_hbm, tail_ref)))
    ]
    for copy in loads:
        copy.start()
    loads[0].wait()
    rad = lax.axis_index("rad")
    count = lax.axis_size("rad")
    keep_low = jnp.where(rad == 0, 0.0, 1.0) * (1.0 / 0.9999)
    keep_high = jnp.where(rad == count - 1, 0.0, 1.0) * (1.0 / 0.9999)
    for s in range(ORD):
        for k in range(2):
            at = (k * ORD + s) * LAT
            edges[0, at:at + LAT, :] = take(edge_ref[0, s, 1 + 3 * k:4 + 3 * k])
            edges[1, at:at + LAT, :] = take(edge_ref[1, s, 3 * k:3 * k + 3])
        scales[0, 8 * s:8 * s + 8, :] = value(edge_ref[0, s, 0])
        scales[1, 8 * s:8 * s + 8, :] = value(edge_ref[1, s, SCALE])
    for e in range(2):
        turn_scales(scales.at[e], turned.at[e])
    place = place_of_latitudes()
    turn_edges = turner(4)

    @pl.loop(0, LAT // GROUP)
    def _(n):
        for j in range(GROUP):
            i = n * GROUP + j
            at, row = place(i)
            below = jnp.exp(LN2 * turned[0, pl.ds(row, 1), :]) * keep_low
            above = jnp.exp(LN2 * turned[1, pl.ds(row, 1), :]) * keep_high
            ends = turn_edges([edges[e, pl.ds(at, 32, stride=LAT), :] for e in range(2)])
            outer[pl.ds(i, 32, stride=LAT), :] = ends[:, :128] * below
            outer[pl.ds(32 * LAT + i, 32, stride=LAT), :] = ends[:, 128:] * above

    for copy in loads[1:]:
        copy.wait()

    def level(eo, c, p, r):
        tail = 2 * p + c
        if r < 0:
            ref, at = outer, eo * 16 + (r + 2) * 8
        elif r < 2:
            ref, at = inner, 64 + eo * 16 + r * 8
        elif r < 6:
            ref, at = inner, eo * 32 + (r - 2) * 8
        elif r < 8:
            ref, at = inner, 96 + eo * 16 + (r - 6) * 8
        else:
            ref, at = outer, 32 + eo * 16 + (r - 8) * 8
        return ref[pl.ds(pl.multiple_of((at + tail) * LAT, 8), LAT), :]

    def out_copy(p, side):
        columns = pl.ds(side * HALF, HALF)
        return pltpu.make_async_copy(result.at[p, :, :, :, columns], out_ref.at[p, :, :, :, columns], sem.at[p, side])

    def potential(p):
        totals = []
        for eo in range(2):
            parts = [jnp.concatenate([level(eo, c, p, r) for r in range(-2, LEV + 2)], axis=0) for c in range(2)]
            high, low = split(jnp.concatenate(parts, axis=1))
            main = jnp.dot(jnp.concatenate([high, low, high], axis=1), main_ref[eo], preferred_element_type=F32)
            tail = jnp.dot(jnp.concatenate([high, low], axis=1), tail_ref[eo], preferred_element_type=F32)
            totals.append(jnp.concatenate([main, tail[:, :128] + tail[:, 128:]], axis=1))
        for side in range(2):
            total = totals[0] + totals[1] if side == 0 else totals[0] - totals[1]
            columns = pl.ds(side * HALF, HALF)
            for r in range(LEV):
                level_of = [total[(r + d) * LAT:(r + d + 1) * LAT] for d in range(5)]
                result[p, 0, r, :, columns] = level_of[2].astype(BF16)
                slope = (level_of[0] - level_of[4]) * (1.0 / 12.0) + (level_of[3] - level_of[1]) * (8.0 / 12.0)
                result[p, 1, r, :, columns] = slope.astype(BF16)
            out_copy(p, side).start()

    @pl.loop(0, POT)
    def _(p):
        potential(p)

    for p in range(POT):
        for side in range(2):
            out_copy(p, side).wait()


def body(coefficients, order_of_slot):
    vmem = pl.BlockSpec(memory_space=pltpu.VMEM)
    anywhere = pl.BlockSpec(memory_space=pl.ANY)
    peers = len(OFFSETS)
    inner, edge, main, tail = pl.pallas_call(
        exchange_kernel,
        out_shape=[
            jax.ShapeDtypeStruct((128 * LAT, 128), F32),
            jax.ShapeDtypeStruct((2, ORD, EDGE, 8, 128), jnp.int16),
            jax.ShapeDtypeStruct((2, 3 * LDEG, 256), BF16),
            jax.ShapeDtypeStruct((2, 2 * LDEG, 256), BF16),
        ],
        in_specs=[pl.BlockSpec(memory_space=pltpu.SMEM), vmem, anywhere],
        out_specs=[anywhere] * 4,
        scratch_shapes=[
            pltpu.VMEM((2, 3 * LDEG, 256), BF16),
            pltpu.VMEM((2, 2 * LDEG, 256), BF16),
            pltpu.VMEM((SLOTS, LEV, POT, 2, LDEG), BF16),
            pltpu.VMEM((ORD, UNITS, 8, 128), jnp.int16),
            pltpu.VMEM((3, PAIRS * STEP, 128), F32),
            pltpu.VMEM((3, PAIRS * STEP, 128), F32),
            pltpu.VMEM((3, PAIRS, STEP + LDEG, 128), BF16),
            pltpu.VMEM((3, PAIRS, STEP + LDEG, 128), BF16),
            pltpu.VMEM((3, SLOTS * 64, 128), F32),
            pltpu.VMEM((ORD, UNITS, 8, 128), jnp.int16),
            pltpu.VMEM((64 * LAT, 128), F32),
            pltpu.VMEM((2, 32 * LAT, 128), F32),
            pltpu.VMEM((128, 128), F32),
            pltpu.VMEM((NLAT, 128), F32),
            pltpu.VMEM((128 * LAT, 128), F32),
            pltpu.SemaphoreType.DMA((POT * LEV,)),
            pltpu.SemaphoreType.DMA,
            pltpu.SemaphoreType.DMA((2,)),
            pltpu.SemaphoreType.DMA((peers,)),
            pltpu.SemaphoreType.DMA((peers,)),
            pltpu.SemaphoreType.DMA((ORD,)),
            pltpu.SemaphoreType.DMA((ORD,)),
            pltpu.SemaphoreType.DMA((ORD,)),
            pltpu.SemaphoreType.DMA((ORD,)),
        ],
        compiler_params=pltpu.CompilerParams(collective_id=0, has_side_effects=True),
    )(order_of_slot, order_of_slot.reshape(1, LDEG), coefficients)
    return pl.pallas_call(
        fourier_kernel,
        out_shape=jax.ShapeDtypeStruct((POT, 2, LEV, LAT, NLON), BF16),
        in_specs=[anywhere] * 4,
        out_specs=anywhere,
        scratch_shapes=[
            pltpu.VMEM((128 * LAT, 128), F32),
            pltpu.VMEM((2, ORD, EDGE, 8, 128), jnp.int16),
            pltpu.VMEM((2, 3 * LDEG, 256), BF16),
            pltpu.VMEM((2, 2 * LDEG, 256), BF16),
            pltpu.VMEM((2, 32 * LAT, 128), F32),
            pltpu.VMEM((2, 128, 128), F32),
            pltpu.VMEM((2, NLAT, 128), F32),
            pltpu.VMEM((64 * LAT, 128), F32),
            pltpu.VMEM((POT, 2, LEV, LAT, NLON), BF16),
            pltpu.SemaphoreType.DMA((4,)),
            pltpu.SemaphoreType.DMA((POT, 2)),
        ],
    )(inner, edge, main, tail)


def solution(mesh):
    return jax.shard_map(
        body,
        mesh=mesh,
        in_specs=(P(None, "rad", "ord", None, None), P()),
        out_specs=P(None, None, "rad", "ord", None),
        check_vma=False,
    )
```
